32 devices in a mesh: freq: 2 (over x), row: 16 (over z, y, core).
Axes of the slice: x: 2, y: 2, z: 4, core: 2. Of those that a mesh axis runs over, the one named last changes fastest.
Arguments:
- data_real: bfloat16 [16384, 8192], P(('freq', 'row')), parts along dimension 0, may hold values from -6 to 6
- data_imag: bfloat16 [16384, 8192], P(('freq', 'row')), parts along dimension 0, may hold values from -6 to 6
- counts: int32 [8, 8], replicated, may hold values from 0 to 4
- source_cols: int32 [128], replicated, may hold values from 0 to 8191, as said below
Outputs:
- pred_real: float32 [16384, 128], P(('freq', 'row')), parts along dimension 0
- pred_imag: float32 [16384, 128], P(('freq', 'row')), parts along dimension 0
The draws below stay inside these ranges and needn't reach their ends.
There are 2 independent parts, one for each index of `freq`. The reference program is written for one: setup_inputs(seed, part) draws one part's arguments, and reference() takes and returns one part's arrays. A program takes and returns all parts, laid end to end along the dimension named above; an argument that names none is the same for every part. Nothing has to cross between parts.
Inputs may be any that keep to these rules, and one draw needn't show every extreme that they name: `source_cols`: 128 distinct grid points; 0 and 8191 are always among them.
All inputs are finite; a program needn't handle non-finite values.
Results may differ from the reference program's by a relative error of at most 0.0029.
Values may be sent and summed in bfloat16 or wider, within the bound.
A program may use at most 128 MiB of HBM per device.

```python
import jax
import jax.numpy as jnp
from jax import lax

N = 8192
SRC = 128
TILES = 8


def draw_source_cols(key, part):
    inner = jax.random.permutation(jax.random.fold_in(key, 11), N - 2)[:SRC - 2] + 1
    both = jnp.concatenate([jnp.array([0, N - 1], jnp.int32), inner.astype(jnp.int32)])
    order = jax.random.permutation(jax.random.fold_in(key, 12), SRC)
    return both[order]


def place_ends(values, rng, smallest, largest):
    shape = values.shape
    index_at = [jax.random.randint(jax.random.fold_in(rng, axis), (), 0, shape[axis]) for axis in range(len(shape))]
    values = values.at[tuple(index_at)].set(smallest)
    longest = shape.index(max(shape))
    index_at[longest] = (index_at[longest] + 1) % shape[longest]
    return values.at[tuple(index_at)].set(largest)


def strengthened(drawn, own_key, source, target, blocks, factor):
    def block_of(dim):
        return (jnp.arange(drawn.shape[dim]) // (drawn.shape[dim] // blocks)).reshape((-1,) + (1,) * (drawn.ndim - 1 - dim))

    one_side = jax.random.permutation(own_key, blocks)[block_of(target)]
    far = (block_of(target) + blocks // 2) % blocks
    return jnp.where((block_of(source) == one_side) | (block_of(source) == far), factor * drawn, drawn)


def level_of(own_key, dims, cuts, least, high):
    def one(position, shards_of):
        draws = jax.random.uniform(jax.random.fold_in(jax.random.fold_in(own_key, 6), position), (shards_of,), jnp.float32, least / len(cuts), high / len(cuts))
        return jnp.repeat(jnp.exp(draws), dims[position] // shards_of).reshape((-1,) + (1,) * (len(dims) - position - 1))

    factor_of = one(*cuts[0])
    for cut in cuts[1:]:
        factor_of = factor_of * one(*cut)
    return factor_of


def noise_with(key, shape, deviation, most, pieces, heavy, kind=jnp.bfloat16):
    entries = deviation * jax.random.normal(key, shape, jnp.float32)
    if pieces:
        entries = entries * level_of(key, shape, pieces, -0.22, 0.18)
    return jnp.clip(strengthened(entries, jax.random.fold_in(key, 3), *heavy), -most, most).astype(kind)


def setup_inputs(seed: int = 0, part: int = 0) -> dict:
    streams_of = jax.random.split(jax.random.key(seed), 5)
    part_keys = jax.random.split(jax.random.fold_in(streams_of[4], part), 5)
    data_real = noise_with(part_keys[0], (N, N), 1.0, 6.0, ((0, 16),), (0, 1, 16, 2.0))
    data_imag = noise_with(part_keys[1], (N, N), 1.0, 6.0, ((0, 16),), (0, 1, 16, 2.0))
    counts = place_ends(jax.random.randint(streams_of[2], (TILES, TILES), 0, 5), jax.random.fold_in(streams_of[2], 1), 0, 4).astype(jnp.int32)
    source_cols = draw_source_cols(jax.random.fold_in(streams_of[4], 71), part)
    return {"data_real": data_real, "data_imag": data_imag, "counts": counts, "source_cols": source_cols}


def symmetrize(data_real, data_imag, counts, row_ids):
    width = data_real.shape[1]
    tile = width // TILES
    table = counts.astype(jnp.float32)
    col_tiles = jnp.arange(width, dtype=jnp.int32) // tile
    row_tiles = row_ids // tile
    forward = table[row_tiles][:, col_tiles]
    backward = table.T[row_tiles][:, col_tiles]
    denom = jnp.maximum(forward + backward, 1.0)
    results = []
    for data in (data_real, data_imag):
        own = data[row_ids, :].astype(jnp.float32)
        mirror = data[:, row_ids].T.astype(jnp.float32)
        results.append(((forward * own + backward * mirror) / denom).astype(jnp.bfloat16))
    return (results[0], results[1])

def reference(data_real, data_imag, counts, source_cols):
    width = data_real.shape[0]
    tile = width // TILES
    src_real, src_imag = symmetrize(data_real, data_imag, counts, source_cols.astype(jnp.int32))
    panel_real = src_real.T
    panel_imag = src_imag.T
    factor = -1.0 / jnp.sqrt(jnp.float32(width))

    def block(index):
        row_ids = (index * tile + jnp.arange(tile, dtype=jnp.int32)).astype(jnp.int32)
        sym_real, sym_imag = symmetrize(data_real, data_imag, counts, row_ids)
        real = jnp.dot(sym_real, panel_real, preferred_element_type=jnp.float32) - jnp.dot(sym_imag, panel_imag, preferred_element_type=jnp.float32)
        imag = jnp.dot(sym_real, panel_imag, preferred_element_type=jnp.float32) + jnp.dot(sym_imag, panel_real, preferred_element_type=jnp.float32)
        return (factor * real, factor * imag)
    real, imag = lax.map(block, jnp.arange(TILES, dtype=jnp.int32))
    count = source_cols.shape[0]
    return (real.reshape(width, count), imag.reshape(width, count))
```

```python
import math

import jax
import jax.numpy as jnp
from jax import lax
from jax.experimental import pallas as pl
from jax.experimental.pallas import tpu as pltpu
from jax.sharding import PartitionSpec as P

TILES = 8
NZ = 4
CHIPS = 8
SLOTS = 32
MESH = pl.DeviceIdType.MESH
NN = (((1,), (0,)), ((), ()))
bf16 = jnp.bfloat16
f32 = jnp.float32


def dot(a, b, dims=NN):
    return lax.dot_general(a, b, dims, preferred_element_type=f32)


class Plan:
    def __init__(self, rows, sources):
        self.rows = rows
        self.sources = sources
        self.pair = 2 * sources
        self.panel_a = rows * 5 // 8
        self.sum_a = self.pair * 5 // 8


def fused_kernel(plan, counts_ref, cols_row_ref, cols_col_ref, dr_hbm, di_hbm, real_ref, imag_ref,
                 d, rows_out, rows_kept, rows_got, rows_all, own, panels, pt, sums_out, sums_got, sums,
                 ya, la, ra, lb, rb, yb, acc, total,
                 load_sem, rs_send, rs_recv, ra_send, ra_recv,
                 g_send, g_recv, xs_send, xs_recv, y_send, y_recv, la_send, la_recv, ra2_send, ra2_recv,
                 lb_send, lb_recv, rb_send, rb_recv, yb_send, yb_recv):
    R, S, PAIR = plan.rows, plan.sources, plan.pair
    PA, SA = plan.panel_a, plan.sum_a
    me = lax.axis_index("row")
    core = lax.rem(me, 2)
    chip = me // 2
    y = lax.rem(chip, 2)
    z = chip // 2
    sibling = chip * 2 + (1 - core)

    def dev(k):
        return {"row": k * 2 + core}

    sib = {"row": sibling}
    across = {"row": (z * 2 + (1 - y)) * 2 + core}
    rightd = {"row": ((z + 1) * 2 + y) * 2 + core}
    leftd = {"row": ((z - 1) * 2 + y) * 2 + core}

    def flip(k, m):
        kz, ky = k // 2, lax.rem(k, 2)
        mz, my = m // 2, lax.rem(m, 2)
        hz, lz = kz // 2, lax.rem(kz, 2)
        hm, lm = mz // 2, lax.rem(mz, 2)
        return (lax.rem(hz + hm, 2) * 2 + lax.rem(lz + lm, 2)) * 2 + lax.rem(ky + my, 2)

    def load(q, k):
        src = (dr_hbm, di_hbm)[q]
        return pltpu.make_async_copy(
            src.at[:, pl.ds(pl.multiple_of(k * 2 * R, 2 * R), 2 * R)], d.at[q, k], load_sem.at[q, k])

    @pl.loop(0, CHIPS)
    def _(i):
        k = flip(chip, CHIPS - 1 - i)
        load(0, k).start()
        load(1, k).start()

    def remote(src, dst, ssem, rsem, where):
        return pltpu.make_async_remote_copy(
            src_ref=src, dst_ref=dst, send_sem=ssem, recv_sem=rsem, device_id=where, device_id_type=MESH)

    barrier = pltpu.get_barrier_semaphore()
    pl.semaphore_signal(barrier, inc=1, device_id=sib, device_id_type=MESH)

    @pl.loop(1, CHIPS)
    def _(m):
        pl.semaphore_signal(barrier, inc=1, device_id=dev(flip(chip, m)), device_id_type=MESH)

    def chip_of(cols):
        return sum((cols >= t * 2 * R).astype(jnp.int32) for t in range(1, CHIPS))

    cols_row, cols_col = cols_row_ref[...], cols_col_ref[...]
    chip_row, chip_col = chip_of(cols_row), chip_of(cols_col)
    same = (jnp.broadcast_to(chip_row, (S, S)) == jnp.broadcast_to(chip_col, (S, S)))
    sub = lax.broadcasted_iota(jnp.int32, (S, S), 0)
    lane = lax.broadcasted_iota(jnp.int32, (S, S), 1)
    rank_row = jnp.sum(jnp.where(same & (sub < lane), 1.0, 0.0), axis=0, keepdims=True)
    rank_col = jnp.sum(jnp.where(same & (lane < sub), 1.0, 0.0), axis=1, keepdims=True)
    slot_row = chip_row.astype(f32) * SLOTS + rank_row
    slot_col = chip_col.astype(f32) * SLOTS + rank_col
    k_iota = lax.broadcasted_iota(jnp.int32, (SLOTS, S), 0).astype(f32)
    mine = jnp.where(slot_row == k_iota + (chip * SLOTS).astype(f32), 1.0, 0.0).astype(bf16)
    at_row = me * R + lax.broadcasted_iota(jnp.int32, (S, R), 1)
    pick = dot(mine, jnp.where(cols_col == at_row, 1.0, 0.0).astype(bf16)).astype(bf16)
    spread = jnp.where(
        slot_col == lax.broadcasted_iota(jnp.int32, (S, CHIPS * SLOTS), 1).astype(f32), 1.0, 0.0).astype(bf16)

    half_other = pl.multiple_of((1 - core) * R, R)
    half_mine = pl.multiple_of(core * R, R)
    pl.semaphore_wait(barrier, CHIPS)

    def to_sibling_rows(k):
        return remote(rows_out.at[k], rows_got.at[k], rs_send.at[k], rs_recv.at[k], sib)

    def to_owner_rows(k):
        return remote(rows_kept.at[k], rows_all.at[chip], ra_send.at[k], ra_recv.at[chip], dev(k))

    @pl.loop(0, CHIPS)
    def _(i):
        k = flip(chip, CHIPS - 1 - i)
        load(0, k).wait()
        load(1, k).wait()
        for q in range(2):
            rows_out[k, q * SLOTS:(q + 1) * SLOTS, :] = dot(pick, d[q, k, :, pl.ds(half_other, R)]).astype(bf16)
        to_sibling_rows(k).start()
        for q in range(2):
            rows_kept[k, q * SLOTS:(q + 1) * SLOTS, :] = dot(pick, d[q, k, :, pl.ds(half_mine, R)]).astype(bf16)

        @pl.when(i > 0)
        def _():
            last = flip(chip, CHIPS - i)
            to_sibling_rows(last).wait_recv()
            rows_kept[last] = rows_kept[last] + rows_got[last]
            to_owner_rows(last).start()

    to_sibling_rows(chip).wait_recv()
    rows_all[chip] = rows_kept[chip] + rows_got[chip]

    own[...] = jnp.zeros_like(own)

    @pl.loop(0, CHIPS)
    def _(k):
        at_col = k * 2 * R + lax.broadcasted_iota(jnp.int32, (2 * R, S), 0)
        take = jnp.where(cols_row == at_col, 1.0, 0.0).astype(bf16)
        own[0] += dot(d[0, k], take)
        own[1] += dot(d[1, k], take)

    tile_me = chip
    w = jnp.zeros((1, S), f32)
    v = jnp.zeros((1, S), f32)
    for t in range(TILES):
        w = jnp.where(chip_row == t, counts_ref[tile_me, t].astype(f32), w)
        v = jnp.where(chip_row == t, counts_ref[t, tile_me].astype(f32), v)
    denom = jnp.maximum(w + v, 1.0)

    @pl.loop(1, CHIPS)
    def _(m):
        k = flip(chip, m)
        remote(rows_all.at[k], rows_all.at[k], ra_send.at[k], ra_recv.at[k], dev(k)).wait_recv()

    for q in range(2):
        mirror = dot(spread, rows_all[:, q * SLOTS:(q + 1) * SLOTS, :].reshape(CHIPS * SLOTS, R)).T
        block = ((w * own[q] + v * mirror) / denom)
        panels[chip, pl.ds(half_mine, R), q * S:(q + 1) * S] = block.astype(bf16)
        side = block.T.astype(bf16)
        pt[0, q * S:(q + 1) * S, :] = side
        pt[1, (1 - q) * S:(2 - q) * S, :] = side if q == 0 else -side

    parts = ((0, PA), (PA, R - PA))

    def block_of(k, c, part):
        off, size = parts[part]
        return panels.at[k, pl.ds(pl.multiple_of(c * R + off, 16), size)]

    def gcopy(k, part, way, where):
        return remote(block_of(k, core, part), block_of(k, core, part), g_send.at[way, part, k], g_recv.at[part, k, core], where)

    def garrived(k, c, part):
        remote(block_of(k, c, part), block_of(k, c, part), g_send.at[0, part, k], g_recv.at[part, k, c], sib).wait_recv()

    def g_right(k, part):
        @pl.when(z < NZ - 1)
        def _():
            gcopy(k, part, 0, rightd).start()

    def g_left(k, part):
        @pl.when(z > 0)
        def _():
            gcopy(k, part, 1, leftd).start()

    def g_across(k, part):
        gcopy(k, part, 2, across).start()

    def g_sib(k, part):
        gcopy(k, part, 3, sib).start()

    for part in range(2):
        g_right(chip, part)
        g_left(chip, part)
        g_across(chip, part)
    for part in range(2):
        g_sib(chip, part)

    chip_y = z * 2 + (1 - y)

    def scale(k):
        f = counts_ref[tile_me, k].astype(f32)
        b = counts_ref[k, tile_me].astype(f32)
        return jnp.full((1, 1), f, f32) / jnp.maximum(jnp.full((1, 1), f + b, f32), 1.0)

    def back(k, half):
        return scale(k) * (dot(pt[0], d[0, k, :, pl.ds(half, R)]) + dot(pt[1], d[1, k, :, pl.ds(half, R)]))

    def sib_sum(k):
        return remote(sums_out.at[k], sums_got.at[k], xs_send.at[k], xs_recv.at[k], sib)

    def in_turn(i):
        return lax.rem(i, NZ) * 2 + jnp.where(i < NZ, 1 - y, y)

    @pl.loop(0, CHIPS)
    def _(i):
        k = in_turn(i)
        sums_out[k] = back(k, half_other).astype(bf16)
        sib_sum(k).start()

    def y_copy(kz):
        return remote(sums.at[kz * 2 + (1 - y), pl.ds(0, SA)], ya.at[kz], y_send.at[kz], y_recv.at[kz], across)

    def own_sum(k):
        value = back(k, half_mine)
        sib_sum(k).wait_recv()
        sums[k] = (value + sums_got[k].astype(f32)).astype(bf16)

    @pl.loop(0, NZ)
    def _(i):
        k = in_turn(i)
        own_sum(k)
        y_copy(i).start()

    def from_line(j):
        @pl.when(z - j >= 0)
        def _():
            k = (z - j) * 2 + y
            garrived(k, core, 0)
            g_right(k, 0)
            g_across(k, 0)
            g_sib(k, 0)
            for ky in (y, 1 - y):
                k = (z - j) * 2 + ky
                garrived(k, core, 1)
                g_right(k, 1)
                g_sib(k, 1)

        @pl.when(z + j <= NZ - 1)
        def _():
            k = (z + j) * 2 + y
            garrived(k, core, 0)
            g_left(k, 0)
            g_across(k, 0)
            g_sib(k, 0)
            for ky in (y, 1 - y):
                k = (z + j) * 2 + ky
                garrived(k, core, 1)
                g_left(k, 1)
                g_sib(k, 1)

    garrived(chip_y, core, 1)
    g_right(chip_y, 1)
    g_left(chip_y, 1)
    g_sib(chip_y, 1)
    from_line(1)

    @pl.loop(NZ, CHIPS)
    def _(i):
        own_sum(in_turn(i))

    def la_copy(kz):
        return remote(sums.at[kz * 2 + y, pl.ds(0, SA)], la.at[kz], la_send.at[kz], la_recv.at[kz], rightd)

    def ra_copy(kz):
        return remote(sums.at[kz * 2 + y, pl.ds(0, SA)], ra.at[kz], ra2_send.at[kz], ra2_recv.at[kz], leftd)

    def lb_copy(k):
        return remote(sums.at[k, pl.ds(SA, PAIR - SA)], lb.at[k], lb_send.at[k], lb_recv.at[k], rightd)

    def rb_copy(k):
        return remote(sums.at[k, pl.ds(SA, PAIR - SA)], rb.at[k], rb_send.at[k], rb_recv.at[k], leftd)

    def add_a(k, term):
        sums[k, :SA, :] = (sums[k, :SA, :].astype(f32) + term.astype(f32)).astype(bf16)

    def add_b(k, term):
        sums[k, SA:, :] = (sums[k, SA:, :].astype(f32) + term.astype(f32)).astype(bf16)

    def pass_on(kz, has_before, copy_a, buf_a, copy_b, buf_b):
        for ky in (y, 1 - y):
            k = kz * 2 + ky

            @pl.when(has_before)
            def _():
                copy_b(k).wait_recv()
                add_b(k, buf_b[k])

            copy_b(k).start()
        k = kz * 2 + y
        y_copy(kz).wait_recv()
        add_a(k, ya[kz])

        @pl.when(has_before)
        def _():
            copy_a(kz).wait_recv()
            add_a(k, buf_a[kz])

        copy_a(kz).start()

    def reduce_step(t):
        @pl.when(z + t <= NZ - 1)
        def _():
            pass_on(z + t, z > 0, la_copy, la, lb_copy, lb)

        @pl.when(z - t >= 0)
        def _():
            pass_on(z - t, z < NZ - 1, ra_copy, ra, rb_copy, rb)

    total[...] = jnp.zeros_like(total)

    def forward(k):
        for c in (1 - core,):
            garrived(k, c, 0)
            garrived(k, c, 1)
        panel = panels[k]
        s = scale(k)
        for q in range(2):
            total[q] += s * dot(d[q, k], panel)

    def forward_line(j):
        @pl.when(z - j >= 0)
        def _():
            forward((z - j) * 2 + y)

        @pl.when(z + j <= NZ - 1)
        def _():
            forward((z + j) * 2 + y)

    reduce_step(3)
    from_line(2)
    forward(chip)
    reduce_step(2)
    forward_line(1)
    from_line(3)
    reduce_step(1)

    for ky in (1 - y, y):
        k = z * 2 + ky

        @pl.when(z > 0)
        def _():
            lb_copy(k).wait_recv()
            add_b(k, lb[k])

        @pl.when(z < NZ - 1)
        def _():
            rb_copy(k).wait_recv()
            add_b(k, rb[k])

    def yb_copy():
        return remote(sums.at[z * 2 + (1 - y), pl.ds(SA, PAIR - SA)], yb, yb_send.at[0], yb_recv.at[0], across)

    yb_copy().start()
    forward_line(2)

    def from_across(kz):
        k = kz * 2 + (1 - y)
        garrived(k, core, 0)
        g_sib(k, 0)

    from_across(z)
    for j in range(1, NZ):
        @pl.when(z - j >= 0)
        def _():
            from_across(z - j)

        @pl.when(z + j <= NZ - 1)
        def _():
            from_across(z + j)

    forward_line(3)
    forward(chip_y)
    for j in range(1, NZ):
        @pl.when(z - j >= 0)
        def _():
            forward((z - j) * 2 + (1 - y))

        @pl.when(z + j <= NZ - 1)
        def _():
            forward((z + j) * 2 + (1 - y))

    y_copy(z).wait_recv()
    acc[:SA, :] = sums[chip, :SA, :].astype(f32) + ya[z].astype(f32)

    @pl.when(z > 0)
    def _():
        la_copy(z).wait_recv()
        acc[:SA, :] += la[z].astype(f32)

    @pl.when(z < NZ - 1)
    def _():
        ra_copy(z).wait_recv()
        acc[:SA, :] += ra[z].astype(f32)

    yb_copy().wait_recv()
    acc[SA:, :] = sums[chip, SA:, :].astype(f32) + yb[...].astype(f32)
    factor = -1.0 / math.sqrt(CHIPS * 2 * R)
    real_ref[...] = factor * (total[0, :, :S] - total[1, :, S:] + acc[:S, :].T)
    imag_ref[...] = factor * (total[0, :, S:] + total[1, :, :S] + acc[S:, :].T)

    @pl.loop(0, CHIPS)
    def _(k):
        to_sibling_rows(k).wait_send()
        sib_sum(k).wait_send()

    @pl.loop(1, CHIPS)
    def _(m):
        to_owner_rows(flip(chip, m)).wait_send()

    @pl.loop(0, NZ)
    def _(kz):
        y_copy(kz).wait_send()
        for part in range(2):
            for ky in (0, 1):
                gcopy(kz * 2 + ky, part, 3, sib).wait_send()
        gcopy(kz * 2 + y, 0, 2, across).wait_send()

        @pl.when((kz <= z) & (z < NZ - 1))
        def _():
            gcopy(kz * 2 + y, 0, 0, rightd).wait_send()
            gcopy(kz * 2, 1, 0, rightd).wait_send()
            gcopy(kz * 2 + 1, 1, 0, rightd).wait_send()

        @pl.when((kz >= z) & (z > 0))
        def _():
            gcopy(kz * 2 + y, 0, 1, leftd).wait_send()
            gcopy(kz * 2, 1, 1, leftd).wait_send()
            gcopy(kz * 2 + 1, 1, 1, leftd).wait_send()

        @pl.when(kz > z)
        def _():
            la_copy(kz).wait_send()
            lb_copy(kz * 2).wait_send()
            lb_copy(kz * 2 + 1).wait_send()

        @pl.when(kz < z)
        def _():
            ra_copy(kz).wait_send()
            rb_copy(kz * 2).wait_send()
            rb_copy(kz * 2 + 1).wait_send()

    gcopy(chip, 1, 2, across).wait_send()
    yb_copy().wait_send()


def fused(data_real, data_imag, counts, source_cols):
    rows, width = data_real.shape
    S = source_cols.shape[0]
    plan = Plan(rows, S)
    pair, sa = plan.pair, plan.sum_a
    sb = pair - sa
    vmem = pl.BlockSpec(memory_space=pltpu.VMEM)
    smem = pl.BlockSpec(memory_space=pltpu.SMEM)
    hbm = pl.BlockSpec(memory_space=pl.ANY)
    dma = pltpu.SemaphoreType.DMA
    V = pltpu.VMEM

    def kernel(*refs):
        fused_kernel(plan, *refs)

    return pl.pallas_call(
        kernel,
        out_shape=(jax.ShapeDtypeStruct((rows, S), f32),) * 2,
        in_specs=[smem, vmem, vmem, hbm, hbm],
        out_specs=(vmem, vmem),
        scratch_shapes=[
            V((2, CHIPS, rows, 2 * rows), bf16),
            V((CHIPS, 2 * SLOTS, rows), bf16), V((CHIPS, 2 * SLOTS, rows), bf16),
            V((CHIPS, 2 * SLOTS, rows), bf16), V((CHIPS, 2 * SLOTS, rows), bf16),
            V((2, rows, S), f32), V((CHIPS, 2 * rows, pair), bf16), V((2, pair, rows), bf16),
            V((CHIPS, pair, rows), bf16), V((CHIPS, pair, rows), bf16), V((CHIPS, pair, rows), bf16),
            V((NZ, sa, rows), bf16), V((NZ, sa, rows), bf16), V((NZ, sa, rows), bf16),
            V((CHIPS, sb, rows), bf16), V((CHIPS, sb, rows), bf16), V((sb, rows), bf16),
            V((pair, rows), f32), V((2, rows, pair), f32),
            dma((2, CHIPS)), dma((CHIPS,)), dma((CHIPS,)), dma((CHIPS,)), dma((CHIPS,)),
            dma((4, 2, CHIPS)), dma((2, CHIPS, 2)), dma((CHIPS,)), dma((CHIPS,)), dma((NZ,)), dma((NZ,)),
            dma((NZ,)), dma((NZ,)), dma((NZ,)), dma((NZ,)),
            dma((CHIPS,)), dma((CHIPS,)), dma((CHIPS,)), dma((CHIPS,)), dma((1,)), dma((1,)),
        ],
        compiler_params=pltpu.CompilerParams(
            collective_id=0, has_side_effects=True, vmem_limit_bytes=56 << 20),
        cost_estimate=pl.CostEstimate(
            flops=8 * rows * width * pair, bytes_accessed=4 * rows * width, transcendentals=0),
    )(counts, source_cols.reshape(1, S), source_cols.reshape(S, 1), data_real, data_imag)


def generic(data_real, data_imag, counts, source_cols):
    rows, width = data_real.shape
    sources = source_cols.shape[0]
    tile = width // TILES
    factor = -1.0 / math.sqrt(width)
    row0 = lax.axis_index("row") * rows
    table = counts.astype(jnp.float32)
    forward = lax.dynamic_index_in_dim(table, row0 // tile, 0, keepdims=False)
    backward = lax.dynamic_index_in_dim(table, row0 // tile, 1, keepdims=False)
    scale = jnp.repeat(forward / jnp.maximum(forward + backward, 1.0), tile)
    at_row = row0 + jnp.arange(rows, dtype=jnp.int32)
    pick_rows = (source_cols[:, None] == at_row[None, :]).astype(jnp.bfloat16)
    tn = (((0,), (1,)), ((), ()))
    picked = jnp.concatenate([dot(data_real, pick_rows, tn), dot(data_imag, pick_rows, tn)], axis=1)
    mirror = lax.psum_scatter(picked.astype(jnp.bfloat16), "row", scatter_dimension=0, tiled=True)
    own = jnp.concatenate([jnp.take(data_real, source_cols, axis=1), jnp.take(data_imag, source_cols, axis=1)], axis=1)
    tiles = source_cols // tile
    w = jnp.tile(forward[tiles], 2)[None, :]
    v = jnp.tile(backward[tiles], 2)[None, :]
    panel = (w * own.astype(jnp.float32) + v * mirror.astype(jnp.float32)) / jnp.maximum(w + v, 1.0)
    panel = panel.astype(jnp.bfloat16)
    swap = lambda p: jnp.concatenate([-p[:, sources:], p[:, :sources]], axis=1)
    panels = lax.all_gather(panel, "row", axis=0, tiled=True)
    tt = (((0,), (0,)), ((), ()))
    back = scale[:, None] * (dot(data_real, panel, tt) + dot(data_imag, swap(panel), tt))
    back = lax.psum_scatter(back, "row", scatter_dimension=0, tiled=True)
    steps = jnp.stack([
        s * (
            dot(data_real[:, t * tile : (t + 1) * tile], panels[t * tile : (t + 1) * tile])
            + dot(data_imag[:, t * tile : (t + 1) * tile], swap(panels[t * tile : (t + 1) * tile]))
        )
        for t, s in enumerate(scale[::tile])
    ])
    total = factor * (steps.sum(0) + back)
    return total[:, :sources], total[:, sources:]


def solution(mesh):
    n = mesh.shape["row"]

    def body(data_real, data_imag, counts, source_cols):
        rows = data_real.shape[0]
        if rows % 128 == 0 and n == 2 * CHIPS and data_real.shape[1] == n * rows and source_cols.shape[0] % 128 == 0:
            chips = source_cols // (2 * rows)
            held = jnp.sum((chips[:, None] == jnp.arange(CHIPS)[None, :]).astype(jnp.int32), axis=0)
            return lax.cond(
                jnp.max(held) <= SLOTS, fused, generic, data_real, data_imag, counts, source_cols)
        return generic(data_real, data_imag, counts, source_cols)

    placed = (P(("freq", "row"), None), P(("freq", "row"), None), P(), P())
    return jax.shard_map(
        body,
        mesh=mesh,
        in_specs=placed,
        out_specs=(P(("freq", "row"), None), P(("freq", "row"), None)),
        check_vma=False,
    )
```

```python
import math

import jax
import jax.numpy as jnp
from jax import lax
from jax.experimental import pallas as pl
from jax.experimental.pallas import tpu as pltpu
from jax.sharding import PartitionSpec as P

TILES = 8
NZ = 4
CHIPS = 8
SLOTS = 32
MESH = pl.DeviceIdType.MESH
NN = (((1,), (0,)), ((), ()))
bf16 = jnp.bfloat16
f32 = jnp.float32


def dot(a, b, dims=NN):
    return lax.dot_general(a, b, dims, preferred_element_type=f32)


class Plan:
    def __init__(self, rows, sources):
        self.rows = rows
        self.sources = sources
        self.pair = 2 * sources
        self.panel_a = rows * 5 // 8
        self.sum_a = self.pair * 5 // 8


def fused_kernel(plan, counts_ref, cols_ref, dr_hbm, di_hbm, real_ref, imag_ref,
                 d, rows_out, rows_kept, rows_got, rows_all, own, panels, pt, sums_out, sums_got, sums,
                 ya, la, ra, lb, rb, yb, acc, total,
                 load_sem, rs_send, rs_recv, ra_send, ra_recv,
                 g_send, g_recv, xs_send, xs_recv, y_send, y_recv, la_send, la_recv, ra2_send, ra2_recv,
                 lb_send, lb_recv, rb_send, rb_recv, yb_send, yb_recv):
    R, S, PAIR = plan.rows, plan.sources, plan.pair
    PA, SA = plan.panel_a, plan.sum_a
    me = lax.axis_index("row")
    core = lax.rem(me, 2)
    chip = me // 2
    y = lax.rem(chip, 2)
    z = chip // 2
    sibling = chip * 2 + (1 - core)

    def dev(k):
        return {"row": k * 2 + core}

    sib = {"row": sibling}
    across = {"row": (z * 2 + (1 - y)) * 2 + core}
    rightd = {"row": ((z + 1) * 2 + y) * 2 + core}
    leftd = {"row": ((z - 1) * 2 + y) * 2 + core}

    def flip(k, m):
        kz, ky = k // 2, lax.rem(k, 2)
        mz, my = m // 2, lax.rem(m, 2)
        hz, lz = kz // 2, lax.rem(kz, 2)
        hm, lm = mz // 2, lax.rem(mz, 2)
        return (lax.rem(hz + hm, 2) * 2 + lax.rem(lz + lm, 2)) * 2 + lax.rem(ky + my, 2)

    def load(q, k):
        src = (dr_hbm, di_hbm)[q]
        return pltpu.make_async_copy(
            src.at[:, pl.ds(pl.multiple_of(k * 2 * R, 2 * R), 2 * R)], d.at[q, k], load_sem.at[q, k])

    @pl.loop(0, CHIPS)
    def _(i):
        k = flip(chip, CHIPS - 1 - i)
        load(0, k).start()
        load(1, k).start()

    def remote(src, dst, ssem, rsem, where):
        return pltpu.make_async_remote_copy(
            src_ref=src, dst_ref=dst, send_sem=ssem, recv_sem=rsem, device_id=where, device_id_type=MESH)

    barrier = pltpu.get_barrier_semaphore()
    pl.semaphore_signal(barrier, inc=1, device_id=sib, device_id_type=MESH)

    @pl.loop(1, CHIPS)
    def _(m):
        pl.semaphore_signal(barrier, inc=1, device_id=dev(flip(chip, m)), device_id_type=MESH)

    def chip_of(cols):
        return sum((cols >= t * 2 * R).astype(jnp.int32) for t in range(1, CHIPS))

    cols_row = cols_ref[...]
    cols_col = jnp.broadcast_to(cols_row.astype(f32), (S, S)).T.astype(jnp.int32)[:, :1]
    chip_row, chip_col = chip_of(cols_row), chip_of(cols_col)
    same = (jnp.broadcast_to(chip_row, (S, S)) == jnp.broadcast_to(chip_col, (S, S)))
    sub = lax.broadcasted_iota(jnp.int32, (S, S), 0)
    lane = lax.broadcasted_iota(jnp.int32, (S, S), 1)
    rank_row = jnp.sum(jnp.where(same & (sub < lane), 1.0, 0.0), axis=0, keepdims=True)
    rank_col = jnp.sum(jnp.where(same & (lane < sub), 1.0, 0.0), axis=1, keepdims=True)
    slot_row = chip_row.astype(f32) * SLOTS + rank_row
    slot_col = chip_col.astype(f32) * SLOTS + rank_col
    k_iota = lax.broadcasted_iota(jnp.int32, (SLOTS, S), 0).astype(f32)
    mine = jnp.where(slot_row == k_iota + (chip * SLOTS).astype(f32), 1.0, 0.0).astype(bf16)
    at_row = me * R + lax.broadcasted_iota(jnp.int32, (S, R), 1)
    pick = dot(mine, jnp.where(cols_col == at_row, 1.0, 0.0).astype(bf16)).astype(bf16)
    spread = jnp.where(
        slot_col == lax.broadcasted_iota(jnp.int32, (S, CHIPS * SLOTS), 1).astype(f32), 1.0, 0.0).astype(bf16)

    half_other = pl.multiple_of((1 - core) * R, R)
    half_mine = pl.multiple_of(core * R, R)
    pl.semaphore_wait(barrier, CHIPS)

    def to_sibling_rows(k):
        return remote(rows_out.at[k], rows_got.at[k], rs_send.at[k], rs_recv.at[k], sib)

    def to_owner_rows(k):
        return remote(rows_kept.at[k], rows_all.at[chip], ra_send.at[k], ra_recv.at[chip], dev(k))

    @pl.loop(0, CHIPS)
    def _(i):
        k = flip(chip, CHIPS - 1 - i)
        load(0, k).wait()
        load(1, k).wait()
        for q in range(2):
            rows_out[k, q * SLOTS:(q + 1) * SLOTS, :] = dot(pick, d[q, k, :, pl.ds(half_other, R)]).astype(bf16)
        to_sibling_rows(k).start()
        for q in range(2):
            rows_kept[k, q * SLOTS:(q + 1) * SLOTS, :] = dot(pick, d[q, k, :, pl.ds(half_mine, R)]).astype(bf16)

        @pl.when(i > 0)
        def _():
            last = flip(chip, CHIPS - i)
            to_sibling_rows(last).wait_recv()
            rows_kept[last] = rows_kept[last] + rows_got[last]
            to_owner_rows(last).start()

    to_sibling_rows(chip).wait_recv()
    rows_all[chip] = rows_kept[chip] + rows_got[chip]

    own[...] = jnp.zeros_like(own)

    @pl.loop(0, CHIPS)
    def _(k):
        at_col = k * 2 * R + lax.broadcasted_iota(jnp.int32, (2 * R, S), 0)
        take = jnp.where(cols_row == at_col, 1.0, 0.0).astype(bf16)
        own[0] += dot(d[0, k], take)
        own[1] += dot(d[1, k], take)

    tile_me = chip
    w = jnp.zeros((1, S), f32)
    v = jnp.zeros((1, S), f32)
    for t in range(TILES):
        w = jnp.where(chip_row == t, counts_ref[tile_me, t].astype(f32), w)
        v = jnp.where(chip_row == t, counts_ref[t, tile_me].astype(f32), v)
    denom = jnp.maximum(w + v, 1.0)

    @pl.loop(1, CHIPS)
    def _(m):
        k = flip(chip, m)
        remote(rows_all.at[k], rows_all.at[k], ra_send.at[k], ra_recv.at[k], dev(k)).wait_recv()

    for q in range(2):
        mirror = dot(spread, rows_all[:, q * SLOTS:(q + 1) * SLOTS, :].reshape(CHIPS * SLOTS, R)).T
        block = ((w * own[q] + v * mirror) / denom)
        panels[chip, pl.ds(half_mine, R), q * S:(q + 1) * S] = block.astype(bf16)
        side = block.T.astype(bf16)
        pt[0, q * S:(q + 1) * S, :] = side
        pt[1, (1 - q) * S:(2 - q) * S, :] = side if q == 0 else -side

    parts = ((0, PA), (PA, R - PA))

    def block_of(k, c, part):
        off, size = parts[part]
        return panels.at[k, pl.ds(pl.multiple_of(c * R + off, 16), size)]

    def gcopy(k, part, way, where):
        return remote(block_of(k, core, part), block_of(k, core, part), g_send.at[way, part, k], g_recv.at[part, k, core], where)

    def garrived(k, c, part):
        remote(block_of(k, c, part), block_of(k, c, part), g_send.at[0, part, k], g_recv.at[part, k, c], sib).wait_recv()

    def g_right(k, part):
        @pl.when(z < NZ - 1)
        def _():
            gcopy(k, part, 0, rightd).start()

    def g_left(k, part):
        @pl.when(z > 0)
        def _():
            gcopy(k, part, 1, leftd).start()

    def g_across(k, part):
        gcopy(k, part, 2, across).start()

    def g_sib(k, part):
        gcopy(k, part, 3, sib).start()

    for part in range(2):
        g_right(chip, part)
        g_left(chip, part)
        g_across(chip, part)
    for part in range(2):
        g_sib(chip, part)

    chip_y = z * 2 + (1 - y)

    def scale(k):
        f = counts_ref[tile_me, k].astype(f32)
        b = counts_ref[k, tile_me].astype(f32)
        return jnp.full((1, 1), f, f32) / jnp.maximum(jnp.full((1, 1), f + b, f32), 1.0)

    def back(k, half):
        return scale(k) * (dot(pt[0], d[0, k, :, pl.ds(half, R)]) + dot(pt[1], d[1, k, :, pl.ds(half, R)]))

    def sib_sum(k):
        return remote(sums_out.at[k], sums_got.at[k], xs_send.at[k], xs_recv.at[k], sib)

    def in_turn(i):
        return lax.rem(i, NZ) * 2 + jnp.where(i < NZ, 1 - y, y)

    @pl.loop(0, CHIPS)
    def _(i):
        k = in_turn(i)
        sums_out[k] = back(k, half_other).astype(bf16)
        sib_sum(k).start()

    def y_copy(kz):
        return remote(sums.at[kz * 2 + (1 - y), pl.ds(0, SA)], ya.at[kz], y_send.at[kz], y_recv.at[kz], across)

    def own_sum(k):
        value = back(k, half_mine)
        sib_sum(k).wait_recv()
        sums[k] = (value + sums_got[k].astype(f32)).astype(bf16)

    @pl.loop(0, NZ)
    def _(i):
        k = in_turn(i)
        own_sum(k)
        y_copy(i).start()

    def from_line(j):
        @pl.when(z - j >= 0)
        def _():
            k = (z - j) * 2 + y
            garrived(k, core, 0)
            g_right(k, 0)
            g_across(k, 0)
            g_sib(k, 0)
            for ky in (y, 1 - y):
                k = (z - j) * 2 + ky
                garrived(k, core, 1)
                g_right(k, 1)
                g_sib(k, 1)

        @pl.when(z + j <= NZ - 1)
        def _():
            k = (z + j) * 2 + y
            garrived(k, core, 0)
            g_left(k, 0)
            g_across(k, 0)
            g_sib(k, 0)
            for ky in (y, 1 - y):
                k = (z + j) * 2 + ky
                garrived(k, core, 1)
                g_left(k, 1)
                g_sib(k, 1)

    garrived(chip_y, core, 1)
    g_right(chip_y, 1)
    g_left(chip_y, 1)
    g_sib(chip_y, 1)
    from_line(1)

    @pl.loop(NZ, CHIPS)
    def _(i):
        own_sum(in_turn(i))

    def la_copy(kz):
        return remote(sums.at[kz * 2 + y, pl.ds(0, SA)], la.at[kz], la_send.at[kz], la_recv.at[kz], rightd)

    def ra_copy(kz):
        return remote(sums.at[kz * 2 + y, pl.ds(0, SA)], ra.at[kz], ra2_send.at[kz], ra2_recv.at[kz], leftd)

    def lb_copy(k):
        return remote(sums.at[k, pl.ds(SA, PAIR - SA)], lb.at[k], lb_send.at[k], lb_recv.at[k], rightd)

    def rb_copy(k):
        return remote(sums.at[k, pl.ds(SA, PAIR - SA)], rb.at[k], rb_send.at[k], rb_recv.at[k], leftd)

    def add_a(k, term):
        sums[k, :SA, :] = (sums[k, :SA, :].astype(f32) + term.astype(f32)).astype(bf16)

    def add_b(k, term):
        sums[k, SA:, :] = (sums[k, SA:, :].astype(f32) + term.astype(f32)).astype(bf16)

    def pass_on(kz, has_before, copy_a, buf_a, copy_b, buf_b):
        for ky in (y, 1 - y):
            k = kz * 2 + ky

            @pl.when(has_before)
            def _():
                copy_b(k).wait_recv()
                add_b(k, buf_b[k])

            copy_b(k).start()
        k = kz * 2 + y
        y_copy(kz).wait_recv()
        add_a(k, ya[kz])

        @pl.when(has_before)
        def _():
            copy_a(kz).wait_recv()
            add_a(k, buf_a[kz])

        copy_a(kz).start()

    def reduce_step(t):
        @pl.when(z + t <= NZ - 1)
        def _():
            pass_on(z + t, z > 0, la_copy, la, lb_copy, lb)

        @pl.when(z - t >= 0)
        def _():
            pass_on(z - t, z < NZ - 1, ra_copy, ra, rb_copy, rb)

    total[...] = jnp.zeros_like(total)

    def forward(k):
        for c in (1 - core,):
            garrived(k, c, 0)
            garrived(k, c, 1)
        panel = panels[k]
        s = scale(k)
        for q in range(2):
            total[q] += s * dot(d[q, k], panel)

    def forward_line(j):
        @pl.when(z - j >= 0)
        def _():
            forward((z - j) * 2 + y)

        @pl.when(z + j <= NZ - 1)
        def _():
            forward((z + j) * 2 + y)

    reduce_step(3)
    from_line(2)
    forward(chip)
    reduce_step(2)
    forward_line(1)
    from_line(3)
    reduce_step(1)

    for ky in (1 - y, y):
        k = z * 2 + ky

        @pl.when(z > 0)
        def _():
            lb_copy(k).wait_recv()
            add_b(k, lb[k])

        @pl.when(z < NZ - 1)
        def _():
            rb_copy(k).wait_recv()
            add_b(k, rb[k])

    def yb_copy():
        return remote(sums.at[z * 2 + (1 - y), pl.ds(SA, PAIR - SA)], yb, yb_send.at[0], yb_recv.at[0], across)

    yb_copy().start()
    forward_line(2)

    def from_across(kz):
        k = kz * 2 + (1 - y)
        garrived(k, core, 0)
        g_sib(k, 0)

    from_across(z)
    for j in range(1, NZ):
        @pl.when(z - j >= 0)
        def _():
            from_across(z - j)

        @pl.when(z + j <= NZ - 1)
        def _():
            from_across(z + j)

    forward_line(3)
    forward(chip_y)
    for j in range(1, NZ):
        @pl.when(z - j >= 0)
        def _():
            forward((z - j) * 2 + (1 - y))

        @pl.when(z + j <= NZ - 1)
        def _():
            forward((z + j) * 2 + (1 - y))

    y_copy(z).wait_recv()
    acc[:SA, :] = sums[chip, :SA, :].astype(f32) + ya[z].astype(f32)

    @pl.when(z > 0)
    def _():
        la_copy(z).wait_recv()
        acc[:SA, :] += la[z].astype(f32)

    @pl.when(z < NZ - 1)
    def _():
        ra_copy(z).wait_recv()
        acc[:SA, :] += ra[z].astype(f32)

    yb_copy().wait_recv()
    acc[SA:, :] = sums[chip, SA:, :].astype(f32) + yb[...].astype(f32)
    factor = -1.0 / math.sqrt(CHIPS * 2 * R)
    real_ref[...] = factor * (total[0, :, :S] - total[1, :, S:] + acc[:S, :].T)
    imag_ref[...] = factor * (total[0, :, S:] + total[1, :, :S] + acc[S:, :].T)

    @pl.loop(0, CHIPS)
    def _(k):
        to_sibling_rows(k).wait_send()
        sib_sum(k).wait_send()

    @pl.loop(1, CHIPS)
    def _(m):
        to_owner_rows(flip(chip, m)).wait_send()

    @pl.loop(0, NZ)
    def _(kz):
        y_copy(kz).wait_send()
        for part in range(2):
            for ky in (0, 1):
                gcopy(kz * 2 + ky, part, 3, sib).wait_send()
        gcopy(kz * 2 + y, 0, 2, across).wait_send()

        @pl.when((kz <= z) & (z < NZ - 1))
        def _():
            gcopy(kz * 2 + y, 0, 0, rightd).wait_send()
            gcopy(kz * 2, 1, 0, rightd).wait_send()
            gcopy(kz * 2 + 1, 1, 0, rightd).wait_send()

        @pl.when((kz >= z) & (z > 0))
        def _():
            gcopy(kz * 2 + y, 0, 1, leftd).wait_send()
            gcopy(kz * 2, 1, 1, leftd).wait_send()
            gcopy(kz * 2 + 1, 1, 1, leftd).wait_send()

        @pl.when(kz > z)
        def _():
            la_copy(kz).wait_send()
            lb_copy(kz * 2).wait_send()
            lb_copy(kz * 2 + 1).wait_send()

        @pl.when(kz < z)
        def _():
            ra_copy(kz).wait_send()
            rb_copy(kz * 2).wait_send()
            rb_copy(kz * 2 + 1).wait_send()

    gcopy(chip, 1, 2, across).wait_send()
    yb_copy().wait_send()


def fused(data_real, data_imag, counts, source_cols):
    rows, width = data_real.shape
    S = source_cols.shape[0]
    plan = Plan(rows, S)
    pair, sa = plan.pair, plan.sum_a
    sb = pair - sa
    vmem = pl.BlockSpec(memory_space=pltpu.VMEM)
    smem = pl.BlockSpec(memory_space=pltpu.SMEM)
    hbm = pl.BlockSpec(memory_space=pl.ANY)
    dma = pltpu.SemaphoreType.DMA
    V = pltpu.VMEM

    def kernel(*refs):
        fused_kernel(plan, *refs)

    return pl.pallas_call(
        kernel,
        out_shape=(jax.ShapeDtypeStruct((rows, S), f32),) * 2,
        in_specs=[smem, vmem, hbm, hbm],
        out_specs=(vmem, vmem),
        scratch_shapes=[
            V((2, CHIPS, rows, 2 * rows), bf16),
            V((CHIPS, 2 * SLOTS, rows), bf16), V((CHIPS, 2 * SLOTS, rows), bf16),
            V((CHIPS, 2 * SLOTS, rows), bf16), V((CHIPS, 2 * SLOTS, rows), bf16),
            V((2, rows, S), f32), V((CHIPS, 2 * rows, pair), bf16), V((2, pair, rows), bf16),
            V((CHIPS, pair, rows), bf16), V((CHIPS, pair, rows), bf16), V((CHIPS, pair, rows), bf16),
            V((NZ, sa, rows), bf16), V((NZ, sa, rows), bf16), V((NZ, sa, rows), bf16),
            V((CHIPS, sb, rows), bf16), V((CHIPS, sb, rows), bf16), V((sb, rows), bf16),
            V((pair, rows), f32), V((2, rows, pair), f32),
            dma((2, CHIPS)), dma((CHIPS,)), dma((CHIPS,)), dma((CHIPS,)), dma((CHIPS,)),
            dma((4, 2, CHIPS)), dma((2, CHIPS, 2)), dma((CHIPS,)), dma((CHIPS,)), dma((NZ,)), dma((NZ,)),
            dma((NZ,)), dma((NZ,)), dma((NZ,)), dma((NZ,)),
            dma((CHIPS,)), dma((CHIPS,)), dma((CHIPS,)), dma((CHIPS,)), dma((1,)), dma((1,)),
        ],
        compiler_params=pltpu.CompilerParams(
            collective_id=0, has_side_effects=True, vmem_limit_bytes=56 << 20),
        cost_estimate=pl.CostEstimate(
            flops=8 * rows * width * pair, bytes_accessed=4 * rows * width, transcendentals=0),
    )(counts, source_cols.reshape(1, S), data_real, data_imag)


def fits_kernel(span, cols_ref, out_ref):
    cols = cols_ref[...]
    most = jnp.zeros((1, 1), f32)
    for t in range(CHIPS):
        here = (cols >= t * span) & (cols < (t + 1) * span)
        most = jnp.maximum(most, jnp.sum(jnp.where(here, 1.0, 0.0), axis=1, keepdims=True))
    out_ref[0] = (most[0, 0] <= SLOTS).astype(jnp.int32)


def fits(span, source_cols):
    def kernel(cols_ref, out_ref):
        fits_kernel(span, cols_ref, out_ref)

    return pl.pallas_call(
        kernel,
        out_shape=jax.ShapeDtypeStruct((1,), jnp.int32),
        in_specs=[pl.BlockSpec(memory_space=pltpu.VMEM)],
        out_specs=pl.BlockSpec(memory_space=pltpu.SMEM),
    )(source_cols.reshape(1, -1))[0] == 1


def gathered(x):
    return lax.all_gather(x, "row", axis=0, tiled=True)


def scattered(x):
    return lax.psum_scatter(x, "row", scatter_dimension=0, tiled=True)


def swapped(x):
    return lax.all_to_all(x, "row", 0, 0)


def gathered_by_swap(x):
    n = lax.axis_size("row")
    return swapped(jnp.broadcast_to(x[None], (n,) + x.shape)).reshape((-1,) + x.shape[1:])


def scattered_by_swap(x):
    n = lax.axis_size("row")
    return swapped(x.reshape((n, -1) + x.shape[1:])).astype(f32).sum(0)


def crowded(data_real, data_imag, counts, source_cols):
    return generic(data_real, data_imag, counts, source_cols, gathered_by_swap, scattered_by_swap)


def generic(data_real, data_imag, counts, source_cols, gathered=gathered, scattered=scattered):
    rows, width = data_real.shape
    sources = source_cols.shape[0]
    tile = width // TILES
    factor = -1.0 / math.sqrt(width)
    row0 = lax.axis_index("row") * rows
    table = counts.astype(jnp.float32)
    forward = lax.dynamic_index_in_dim(table, row0 // tile, 0, keepdims=False)
    backward = lax.dynamic_index_in_dim(table, row0 // tile, 1, keepdims=False)
    scale = jnp.repeat(forward / jnp.maximum(forward + backward, 1.0), tile)
    at_row = row0 + jnp.arange(rows, dtype=jnp.int32)
    pick_rows = (source_cols[:, None] == at_row[None, :]).astype(jnp.bfloat16)
    tn = (((0,), (1,)), ((), ()))
    picked = jnp.concatenate([dot(data_real, pick_rows, tn), dot(data_imag, pick_rows, tn)], axis=1)
    mirror = scattered(picked.astype(jnp.bfloat16))
    own = jnp.concatenate([jnp.take(data_real, source_cols, axis=1), jnp.take(data_imag, source_cols, axis=1)], axis=1)
    tiles = source_cols // tile
    w = jnp.tile(forward[tiles], 2)[None, :]
    v = jnp.tile(backward[tiles], 2)[None, :]
    panel = (w * own.astype(jnp.float32) + v * mirror.astype(jnp.float32)) / jnp.maximum(w + v, 1.0)
    panel = panel.astype(jnp.bfloat16)
    swap = lambda p: jnp.concatenate([-p[:, sources:], p[:, :sources]], axis=1)
    panels = gathered(panel)
    tt = (((0,), (0,)), ((), ()))
    back = scale[:, None] * (dot(data_real, panel, tt) + dot(data_imag, swap(panel), tt))
    back = scattered(back)
    steps = jnp.stack([
        s * (
            dot(data_real[:, t * tile : (t + 1) * tile], panels[t * tile : (t + 1) * tile])
            + dot(data_imag[:, t * tile : (t + 1) * tile], swap(panels[t * tile : (t + 1) * tile]))
        )
        for t, s in enumerate(scale[::tile])
    ])
    total = factor * (steps.sum(0) + back)
    return total[:, :sources], total[:, sources:]


def solution(mesh):
    n = mesh.shape["row"]

    def body(data_real, data_imag, counts, source_cols):
        rows = data_real.shape[0]
        if rows % 128 == 0 and n == 2 * CHIPS and data_real.shape[1] == n * rows and source_cols.shape[0] % 128 == 0:
            return lax.cond(
                fits(2 * rows, source_cols), fused, crowded, data_real, data_imag, counts, source_cols)
        return generic(data_real, data_imag, counts, source_cols)

    placed = (P(("freq", "row"), None), P(("freq", "row"), None), P(), P())
    return jax.shard_map(
        body,
        mesh=mesh,
        in_specs=placed,
        out_specs=(P(("freq", "row"), None), P(("freq", "row"), None)),
        check_vma=False,
    )
```

```python
import math

import jax
import jax.numpy as jnp
from jax import lax
from jax.experimental import pallas as pl
from jax.experimental.pallas import tpu as pltpu
from jax.sharding import PartitionSpec as P

TILES = 8
NZ = 4
CHIPS = 8
SLOTS = 32
MESH = pl.DeviceIdType.MESH
ORDER = (
    (
        ("own",), ("bo", 3, 1), ("bo", 2, 1), ("bo", 1, 1), ("bo", 0, 1), ("bo", 3, 0), ("bo", 2, 0), ("bo", 1, 0),
        ("bo", 0, 0), ("bm", 3, 1), ("rb", 3, 1), ("bm", 2, 1), ("rb", 2, 1), ("bm", 1, 1), ("g", 0, 1, 0),
        ("g", 0, 0, 1), ("rb", 1, 1), ("bm", 0, 1), ("g", 1, 1, 0), ("g", 1, 0, 1), ("bm", 3, 0), ("rb", 3, 0),
        ("bm", 2, 0), ("rb", 2, 0), ("bm", 1, 0), ("ra", 3), ("rb", 1, 0), ("bm", 0, 0), ("f", 0, 0), ("g", 0, 2, 0),
        ("ra", 2), ("f", 1, 0), ("g", 1, 2, 0), ("f", 0, 1), ("g", 1, 1, 1), ("f", 2, 0), ("ra", 1), ("g", 0, 3, 0),
        ("g", 0, 1, 1), ("g", 1, 3, 0), ("g", 1, 2, 1), ("f", 1, 1), ("f", 3, 0), ("eb",), ("g", 1, 3, 1),
        ("g", 0, 2, 1), ("f", 2, 1), ("g", 0, 3, 1), ("f", 3, 1), ("fb",), ("fa",),
    ),
    (
        ("own",), ("bo", 3, 1), ("bo", 0, 1), ("bo", 2, 1), ("bo", 1, 1), ("bo", 3, 0), ("bo", 0, 0), ("bo", 2, 0),
        ("bo", 1, 0), ("bm", 3, 1), ("bm", 0, 1), ("bm", 2, 1), ("g", 0, 0, 0), ("g", 0, 2, 0), ("g", 0, 1, 1),
        ("bm", 1, 1), ("g", 1, 0, 0), ("g", 1, 2, 0), ("g", 1, 1, 1), ("bm", 3, 0), ("bm", 0, 0), ("rb", 3, 1),
        ("bm", 2, 0), ("bm", 1, 0), ("f", 1, 0), ("g", 0, 3, 0), ("rb", 2, 1), ("g", 1, 3, 0), ("f", 0, 0),
        ("f", 1, 1), ("g", 1, 0, 1), ("g", 1, 2, 1), ("f", 2, 0), ("f", 3, 0), ("rb", 0, 1), ("rb", 3, 0), ("eb",),
        ("g", 0, 0, 1), ("rb", 2, 0), ("g", 1, 3, 1), ("f", 0, 1), ("ra", 3), ("rb", 0, 0), ("g", 0, 2, 1),
        ("f", 2, 1), ("ra", 2), ("ra", 0), ("g", 0, 3, 1), ("f", 3, 1), ("fb",), ("fa",),
    ),
)
NN = (((1,), (0,)), ((), ()))
bf16 = jnp.bfloat16
f32 = jnp.float32


def dot(a, b, dims=NN):
    return lax.dot_general(a, b, dims, preferred_element_type=f32)


class Plan:
    def __init__(self, rows, sources):
        self.rows = rows
        self.sources = sources
        self.pair = 2 * sources
        self.panel_a = rows * 384 // 512
        self.sum_a = self.pair * 144 // 256


def fused_kernel(plan, counts_ref, cols_ref, dr_hbm, di_hbm, real_ref, imag_ref,
                 d, rows_out, rows_kept, rows_got, rows_all, own, panels, pt, sums_out, sums_got, sums, kept,
                 ya, line_a, line_b, yb, acc, total,
                 load_sem, rs_send, rs_recv, ra_send, ra_recv,
                 g_send, g_recv, xs_send, xs_recv, y_send, y_recv, la_send, la_recv, lb_send, lb_recv, yb_send, yb_recv):
    R, S, PAIR = plan.rows, plan.sources, plan.pair
    PA, SA = plan.panel_a, plan.sum_a
    me = lax.axis_index("row")
    core = lax.rem(me, 2)
    chip = me // 2
    y = lax.rem(chip, 2)
    z = chip // 2
    sibling = chip * 2 + (1 - core)

    def dev(k):
        return {"row": k * 2 + core}

    sib = {"row": sibling}

    def flip(k, m):
        kz, ky = k // 2, lax.rem(k, 2)
        mz, my = m // 2, lax.rem(m, 2)
        hz, lz = kz // 2, lax.rem(kz, 2)
        hm, lm = mz // 2, lax.rem(mz, 2)
        return (lax.rem(hz + hm, 2) * 2 + lax.rem(lz + lm, 2)) * 2 + lax.rem(ky + my, 2)

    def load(q, k):
        src = (dr_hbm, di_hbm)[q]
        return pltpu.make_async_copy(
            src.at[:, pl.ds(pl.multiple_of(k * 2 * R, 2 * R), 2 * R)], d.at[q, k], load_sem.at[q, k])

    @pl.loop(0, CHIPS)
    def _(i):
        k = flip(chip, CHIPS - 1 - i)
        load(0, k).start()
        load(1, k).start()

    def remote(src, dst, ssem, rsem, where):
        return pltpu.make_async_remote_copy(
            src_ref=src, dst_ref=dst, send_sem=ssem, recv_sem=rsem, device_id=where, device_id_type=MESH)

    barrier = pltpu.get_barrier_semaphore()
    pl.semaphore_signal(barrier, inc=1, device_id=sib, device_id_type=MESH)

    @pl.loop(1, CHIPS)
    def _(m):
        pl.semaphore_signal(barrier, inc=1, device_id=dev(flip(chip, m)), device_id_type=MESH)

    def chip_of(cols):
        return sum((cols >= t * 2 * R).astype(jnp.int32) for t in range(1, CHIPS))

    cols_row = cols_ref[...]
    cols_col = jnp.broadcast_to(cols_row.astype(f32), (S, S)).T.astype(jnp.int32)[:, :1]
    chip_row, chip_col = chip_of(cols_row), chip_of(cols_col)
    same = (jnp.broadcast_to(chip_row, (S, S)) == jnp.broadcast_to(chip_col, (S, S)))
    sub = lax.broadcasted_iota(jnp.int32, (S, S), 0)
    lane = lax.broadcasted_iota(jnp.int32, (S, S), 1)
    rank_row = jnp.sum(jnp.where(same & (sub < lane), 1.0, 0.0), axis=0, keepdims=True)
    rank_col = jnp.sum(jnp.where(same & (lane < sub), 1.0, 0.0), axis=1, keepdims=True)
    slot_row = chip_row.astype(f32) * SLOTS + rank_row
    slot_col = chip_col.astype(f32) * SLOTS + rank_col
    k_iota = lax.broadcasted_iota(jnp.int32, (SLOTS, S), 0).astype(f32)
    mine = jnp.where(slot_row == k_iota + (chip * SLOTS).astype(f32), 1.0, 0.0).astype(bf16)
    at_row = me * R + lax.broadcasted_iota(jnp.int32, (S, R), 1)
    pick = dot(mine, jnp.where(cols_col == at_row, 1.0, 0.0).astype(bf16)).astype(bf16)
    spread = jnp.where(
        slot_col == lax.broadcasted_iota(jnp.int32, (S, CHIPS * SLOTS), 1).astype(f32), 1.0, 0.0).astype(bf16)

    half_other = pl.multiple_of((1 - core) * R, R)
    half_mine = pl.multiple_of(core * R, R)
    pl.semaphore_wait(barrier, CHIPS)

    def to_sibling_rows(k):
        return remote(rows_out.at[k], rows_got.at[k], rs_send.at[k], rs_recv.at[k], sib)

    def to_owner_rows(k):
        return remote(rows_kept.at[k], rows_all.at[chip], ra_send.at[k], ra_recv.at[chip], dev(k))

    @pl.loop(0, CHIPS)
    def _(i):
        k = flip(chip, CHIPS - 1 - i)
        load(0, k).wait()
        load(1, k).wait()
        for q in range(2):
            rows_out[k, q * SLOTS:(q + 1) * SLOTS, :] = dot(pick, d[q, k, :, pl.ds(half_other, R)]).astype(bf16)
        to_sibling_rows(k).start()
        for q in range(2):
            rows_kept[k, q * SLOTS:(q + 1) * SLOTS, :] = dot(pick, d[q, k, :, pl.ds(half_mine, R)]).astype(bf16)

        @pl.when(i > 0)
        def _():
            last = flip(chip, CHIPS - i)
            to_sibling_rows(last).wait_recv()
            rows_kept[last] = rows_kept[last] + rows_got[last]
            to_owner_rows(last).start()

    to_sibling_rows(chip).wait_recv()
    rows_all[chip] = rows_kept[chip] + rows_got[chip]

    own[...] = jnp.zeros_like(own)

    @pl.loop(0, CHIPS)
    def _(k):
        at_col = k * 2 * R + lax.broadcasted_iota(jnp.int32, (2 * R, S), 0)
        take = jnp.where(cols_row == at_col, 1.0, 0.0).astype(bf16)
        own[0] += dot(d[0, k], take)
        own[1] += dot(d[1, k], take)

    w = jnp.zeros((1, S), f32)
    v = jnp.zeros((1, S), f32)
    for t in range(TILES):
        w = jnp.where(chip_row == t, counts_ref[chip, t].astype(f32), w)
        v = jnp.where(chip_row == t, counts_ref[t, chip].astype(f32), v)
    denom = jnp.maximum(w + v, 1.0)

    @pl.loop(1, CHIPS)
    def _(m):
        k = flip(chip, m)
        remote(rows_all.at[k], rows_all.at[k], ra_send.at[k], ra_recv.at[k], dev(k)).wait_recv()

    for q in range(2):
        mirror = dot(spread, rows_all[:, q * SLOTS:(q + 1) * SLOTS, :].reshape(CHIPS * SLOTS, R)).T
        block = ((w * own[q] + v * mirror) / denom)
        panels[chip, pl.ds(half_mine, R), q * S:(q + 1) * S] = block.astype(bf16)
        side = block.T.astype(bf16)
        pt[0, q * S:(q + 1) * S, :] = side
        pt[1, (1 - q) * S:(2 - q) * S, :] = side if q == 0 else -side

    far = z // 2
    middle = z * (NZ - 1 - z) // 2
    at_end = middle == 0

    def line(u):
        return u + far * (NZ - 1 - 2 * u)

    def chip_at(u, s):
        return line(u) * 2 + (y if s == 0 else 1 - y)

    def turn(table, i):
        u, s = 0, 0
        for n in range(CHIPS):
            (ue, se), (um, sm) = table[0][n], table[1][n]
            here = (i == n).astype(jnp.int32)
            u += here * (ue + middle * (um - ue))
            s += here * (se + middle * (sm - se))
        return line(u) * 2 + y + s * (1 - 2 * y)

    def table(kind):
        return tuple(tuple(t[1:] for t in row if t[0] == kind) for row in ORDER)

    across = {"row": (z * 2 + (1 - y)) * 2 + core}
    parts = ((0, PA), (PA, R - PA))
    ROW_A, ROW_B = pl.ds(0, SA), pl.ds(SA, PAIR - SA)

    def scale(k):
        f = counts_ref[chip, k].astype(f32)
        b = counts_ref[k, chip].astype(f32)
        return jnp.full((1, 1), f, f32) / jnp.maximum(jnp.full((1, 1), f + b, f32), 1.0)

    def block_of(k, c, part):
        off, size = parts[part]
        return panels.at[k, pl.ds(pl.multiple_of(c * R + off, 16), size)]

    def garrived(k, c, part):
        remote(block_of(k, c, part), block_of(k, c, part), g_send.at[0, part, k], g_recv.at[part, k, c], sib).wait_recv()

    def y_copy(kz):
        return remote(sums.at[kz * 2 + (1 - y), ROW_A], ya.at[kz], y_send.at[kz], y_recv.at[kz], across)

    def sib_sum(k):
        return remote(sums_out.at[k], sums_got.at[k], xs_send.at[k], xs_recv.at[k], sib)

    def back(k, half):
        return scale(k) * (dot(pt[0], d[0, k, :, pl.ds(half, R)]) + dot(pt[1], d[1, k, :, pl.ds(half, R)]))

    class Tasks:
        def __init__(self, u):
            self.u = u
            self.sent = []
            self.ends = [w for w in (-1, 1) if 0 <= u + w]

        def toward(self, w):
            return {"row": chip_at(self.u + w, 0) * 2 + core}

        def came(self, w):
            return far if w > 0 else 1 - far

        def start(self, copy, *place):
            copy(*place).start()
            self.sent.append((copy, place))

        def panel_copy(self, u, s, part, way):
            k = chip_at(u, s)
            where = (sib, across, None)[min(3 - way, 2)] or self.toward(2 * way - 1)
            return remote(
                block_of(k, core, part), block_of(k, core, part), g_send.at[way, part, k], g_recv.at[part, k, core], where)

        def own(self):
            for part in range(2):
                for w in self.ends:
                    self.start(self.panel_copy, self.u, 0, part, (w + 1) // 2)
                self.start(self.panel_copy, self.u, 0, part, 2)
            for part in range(2):
                self.start(self.panel_copy, self.u, 0, part, 3)

        def g(self, part, u, s):
            garrived(chip_at(u, s), core, part)
            ways = self.ends if u == self.u else [1 if u < self.u else -1]
            if part == 1 or s == 0:
                for w in ways:
                    if w in self.ends:
                        self.start(self.panel_copy, u, s, part, (w + 1) // 2)
            if part == 0 and s == 0:
                self.start(self.panel_copy, u, s, part, 2)
            self.start(self.panel_copy, u, s, part, 3)

        def a_copy(self, u, w):
            kz = line(u)
            return remote(sums.at[kz * 2 + y, ROW_A], line_a.at[self.came(w), kz], la_send.at[kz], la_recv.at[self.came(w), kz],
                          self.toward(w))

        def b_copy(self, u, s, w):
            k = chip_at(u, s)
            return remote(sums.at[k, ROW_B], line_b.at[self.came(w), k], lb_send.at[k], lb_recv.at[self.came(w), k],
                          self.toward(w))

        def with_a(self, value, kz, w):
            c = self.came(w)
            remote(line_a.at[c, kz], line_a.at[c, kz], la_send.at[kz], la_recv.at[c, kz], sib).wait_recv()
            return value + line_a[c, kz].astype(f32)

        def with_b(self, value, k, w):
            c = self.came(w)
            remote(line_b.at[c, k], line_b.at[c, k], lb_send.at[k], lb_recv.at[c, k], sib).wait_recv()
            return value + line_b[c, k].astype(f32)

        def ra(self, u):
            kz = line(u)
            w = 1 if u > self.u else -1
            y_copy(kz).wait_recv()
            value = kept[kz * 2 + y, :SA, :] + ya[kz].astype(f32)
            if -w in self.ends:
                value = self.with_a(value, kz, w)
            sums[kz * 2 + y, :SA, :] = value.astype(bf16)
            self.start(self.a_copy, u, w)

        def rb(self, u, s):
            k = chip_at(u, s)
            w = 1 if u > self.u else -1
            value = kept[k, SA:, :]
            if -w in self.ends:
                value = self.with_b(value, k, w)
            sums[k, SA:, :] = value.astype(bf16)
            self.start(self.b_copy, u, s, w)

        def ended_b(self, k):
            value = kept[k, SA:, :]
            for w in self.ends:
                value = self.with_b(value, k, -w)
            return value

        def yb_copy(self):
            return remote(sums.at[chip_at(self.u, 1), ROW_B], yb, yb_send.at[0], yb_recv.at[0], across)

        def eb(self):
            k = chip_at(self.u, 1)
            sums[k, SA:, :] = self.ended_b(k).astype(bf16)
            self.start(self.yb_copy)

        def fa(self):
            y_copy(z).wait_recv()
            value = kept[chip, :SA, :] + ya[z].astype(f32)
            for w in self.ends:
                value = self.with_a(value, z, -w)
            acc[:SA, :] = value

        def fb(self):
            value = self.ended_b(chip)
            self.yb_copy().wait_recv()
            acc[SA:, :] = value + yb[...].astype(f32)

    both = (Tasks(0), Tasks(1))

    def slots(kind):
        found = []
        for row in ORDER:
            ahead, lists = [], []
            for t in row:
                if t[0] in ("bo", "bm", "f"):
                    if t[0] == kind:
                        lists.append(ahead)
                    ahead = []
                else:
                    ahead.append(t)
            found.append(lists + [ahead])
        return found

    def run(lists, i):
        for u, row in enumerate(lists):
            for n in range(CHIPS):
                if row[n]:
                    @pl.when((i == n) & (at_end if u == 0 else middle == 1))
                    def _():
                        for t in row[n]:
                            getattr(both[u], t[0])(*t[1:])

    def run_all(lists):
        for u in range(2):
            @pl.when(at_end if u == 0 else middle == 1)
            def _():
                for t in lists[u]:
                    getattr(both[u], t[0])(*t[1:])

    run_all([[("own",)], [("own",)]])
    total[...] = jnp.zeros_like(total)

    @pl.loop(0, CHIPS)
    def _(i):
        k = turn(table("bo"), i)
        sums_out[k] = back(k, half_other).astype(bf16)
        sib_sum(k).start()

    @pl.loop(0, CHIPS)
    def _(i):
        run(slots("bm"), i)
        k = turn(table("bm"), i)
        value = back(k, half_mine)
        sib_sum(k).wait_recv()
        value = value + sums_got[k].astype(f32)
        kept[k] = value

        @pl.when(i < NZ)
        def _():
            sums[k, :SA, :] = value[:SA].astype(bf16)
            y_copy(k // 2).start()

    @pl.loop(0, CHIPS)
    def _(i):
        run(slots("f"), i)
        k = turn(table("f"), i)
        for part in range(2):
            garrived(k, 1 - core, part)
        panel = panels[k]
        size = scale(k)
        for q in range(2):
            total[q] += size * dot(d[q, k], panel)

    run_all([row[CHIPS] for row in slots("f")])
    factor = -1.0 / math.sqrt(CHIPS * 2 * R)
    real_ref[...] = factor * (total[0, :, :S] - total[1, :, S:] + acc[:S, :].T)
    imag_ref[...] = factor * (total[0, :, S:] + total[1, :, :S] + acc[S:, :].T)

    @pl.loop(0, CHIPS)
    def _(k):
        to_sibling_rows(k).wait_send()
        sib_sum(k).wait_send()

    @pl.loop(1, CHIPS)
    def _(m):
        to_owner_rows(flip(chip, m)).wait_send()

    @pl.loop(0, NZ)
    def _(kz):
        y_copy(kz).wait_send()

    for u in range(2):
        @pl.when(at_end if u == 0 else middle == 1)
        def _():
            for copy, place in both[u].sent:
                copy(*place).wait_send()


def fused(data_real, data_imag, counts, source_cols):
    rows, width = data_real.shape
    S = source_cols.shape[0]
    plan = Plan(rows, S)
    pair, sa = plan.pair, plan.sum_a
    sb = pair - sa
    vmem = pl.BlockSpec(memory_space=pltpu.VMEM)
    smem = pl.BlockSpec(memory_space=pltpu.SMEM)
    hbm = pl.BlockSpec(memory_space=pl.ANY)
    dma = pltpu.SemaphoreType.DMA
    V = pltpu.VMEM

    def kernel(*refs):
        fused_kernel(plan, *refs)

    return pl.pallas_call(
        kernel,
        out_shape=(jax.ShapeDtypeStruct((rows, S), f32),) * 2,
        in_specs=[smem, vmem, hbm, hbm],
        out_specs=(vmem, vmem),
        scratch_shapes=[
            V((2, CHIPS, rows, 2 * rows), bf16),
            V((CHIPS, 2 * SLOTS, rows), bf16), V((CHIPS, 2 * SLOTS, rows), bf16),
            V((CHIPS, 2 * SLOTS, rows), bf16), V((CHIPS, 2 * SLOTS, rows), bf16),
            V((2, rows, S), f32), V((CHIPS, 2 * rows, pair), bf16), V((2, pair, rows), bf16),
            V((CHIPS, pair, rows), bf16), V((CHIPS, pair, rows), bf16), V((CHIPS, pair, rows), bf16),
            V((CHIPS, pair, rows), f32),
            V((NZ, sa, rows), bf16), V((2, NZ, sa, rows), bf16), V((2, CHIPS, sb, rows), bf16), V((sb, rows), bf16),
            V((pair, rows), f32), V((2, rows, pair), f32),
            dma((2, CHIPS)), dma((CHIPS,)), dma((CHIPS,)), dma((CHIPS,)), dma((CHIPS,)),
            dma((4, 2, CHIPS)), dma((2, CHIPS, 2)), dma((CHIPS,)), dma((CHIPS,)), dma((NZ,)), dma((NZ,)),
            dma((NZ,)), dma((2, NZ)), dma((CHIPS,)), dma((2, CHIPS)), dma((1,)), dma((1,)),
        ],
        compiler_params=pltpu.CompilerParams(
            collective_id=0, has_side_effects=True, vmem_limit_bytes=56 << 20),
        cost_estimate=pl.CostEstimate(
            flops=8 * rows * width * pair, bytes_accessed=4 * rows * width, transcendentals=0),
    )(counts, source_cols.reshape(1, S), data_real, data_imag)


def fits_kernel(span, cols_ref, out_ref):
    cols = cols_ref[...]
    most = jnp.zeros((1, 1), f32)
    for t in range(CHIPS):
        here = (cols >= t * span) & (cols < (t + 1) * span)
        most = jnp.maximum(most, jnp.sum(jnp.where(here, 1.0, 0.0), axis=1, keepdims=True))
    out_ref[0] = (most[0, 0] <= SLOTS).astype(jnp.int32)


def fits(span, source_cols):
    def kernel(cols_ref, out_ref):
        fits_kernel(span, cols_ref, out_ref)

    return pl.pallas_call(
        kernel,
        out_shape=jax.ShapeDtypeStruct((1,), jnp.int32),
        in_specs=[pl.BlockSpec(memory_space=pltpu.VMEM)],
        out_specs=pl.BlockSpec(memory_space=pltpu.SMEM),
    )(source_cols.reshape(1, -1))[0] == 1


def gathered(x):
    return lax.all_gather(x, "row", axis=0, tiled=True)


def scattered(x):
    return lax.psum_scatter(x, "row", scatter_dimension=0, tiled=True)


def swapped(x):
    return lax.all_to_all(x, "row", 0, 0)


def gathered_by_swap(x):
    n = lax.axis_size("row")
    return swapped(jnp.broadcast_to(x[None], (n,) + x.shape)).reshape((-1,) + x.shape[1:])


def scattered_by_swap(x):
    n = lax.axis_size("row")
    return swapped(x.reshape((n, -1) + x.shape[1:])).astype(f32).sum(0)


def crowded(data_real, data_imag, counts, source_cols):
    return generic(data_real, data_imag, counts, source_cols, gathered_by_swap, scattered_by_swap)


def generic(data_real, data_imag, counts, source_cols, gathered=gathered, scattered=scattered):
    rows, width = data_real.shape
    sources = source_cols.shape[0]
    tile = width // TILES
    factor = -1.0 / math.sqrt(width)
    row0 = lax.axis_index("row") * rows
    table = counts.astype(jnp.float32)
    forward = lax.dynamic_index_in_dim(table, row0 // tile, 0, keepdims=False)
    backward = lax.dynamic_index_in_dim(table, row0 // tile, 1, keepdims=False)
    scale = jnp.repeat(forward / jnp.maximum(forward + backward, 1.0), tile)
    at_row = row0 + jnp.arange(rows, dtype=jnp.int32)
    pick_rows = (source_cols[:, None] == at_row[None, :]).astype(jnp.bfloat16)
    tn = (((0,), (1,)), ((), ()))
    picked = jnp.concatenate([dot(data_real, pick_rows, tn), dot(data_imag, pick_rows, tn)], axis=1)
    mirror = scattered(picked.astype(jnp.bfloat16))
    own = jnp.concatenate([jnp.take(data_real, source_cols, axis=1), jnp.take(data_imag, source_cols, axis=1)], axis=1)
    tiles = source_cols // tile
    w = jnp.tile(forward[tiles], 2)[None, :]
    v = jnp.tile(backward[tiles], 2)[None, :]
    panel = (w * own.astype(jnp.float32) + v * mirror.astype(jnp.float32)) / jnp.maximum(w + v, 1.0)
    panel = panel.astype(jnp.bfloat16)
    swap = lambda p: jnp.concatenate([-p[:, sources:], p[:, :sources]], axis=1)
    panels = gathered(panel)
    tt = (((0,), (0,)), ((), ()))
    back = scale[:, None] * (dot(data_real, panel, tt) + dot(data_imag, swap(panel), tt))
    back = scattered(back)
    steps = jnp.stack([
        s * (
            dot(data_real[:, t * tile : (t + 1) * tile], panels[t * tile : (t + 1) * tile])
            + dot(data_imag[:, t * tile : (t + 1) * tile], swap(panels[t * tile : (t + 1) * tile]))
        )
        for t, s in enumerate(scale[::tile])
    ])
    total = factor * (steps.sum(0) + back)
    return total[:, :sources], total[:, sources:]


def solution(mesh):
    n = mesh.shape["row"]

    def body(data_real, data_imag, counts, source_cols):
        rows = data_real.shape[0]
        if rows % 128 == 0 and n == 2 * CHIPS and data_real.shape[1] == n * rows and source_cols.shape[0] % 128 == 0:
            return lax.cond(
                fits(2 * rows, source_cols), fused, crowded, data_real, data_imag, counts, source_cols)
        return generic(data_real, data_imag, counts, source_cols)

    placed = (P(("freq", "row"), None), P(("freq", "row"), None), P(), P())
    return jax.shard_map(
        body,
        mesh=mesh,
        in_specs=placed,
        out_specs=(P(("freq", "row"), None), P(("freq", "row"), None)),
        check_vma=False,
    )
```

```python
import math

import jax
import jax.numpy as jnp
from jax import lax
from jax.experimental import pallas as pl
from jax.experimental.pallas import tpu as pltpu
from jax.sharding import PartitionSpec as P

TILES = 8
NZ = 4
CHIPS = 8
SLOTS = 32
MESH = pl.DeviceIdType.MESH
ORDER = (
    (
        ("own", 0), ("own", 1), ("bo", 3, 1), ("bo", 1, 1), ("bo", 2, 1), ("bo", 3, 0), ("g", 0, 1, 0), ("bo", 0, 0),
        ("bo", 0, 1), ("bo", 2, 0), ("bo", 1, 0), ("bm", 3, 1), ("g", 1, 0, 1), ("bm", 3, 0), ("bm", 2, 1),
        ("rb", 3, 1), ("rb", 2, 1), ("rb", 3, 0), ("bm", 1, 1), ("g", 0, 2, 0), ("g", 1, 1, 1), ("g", 0, 0, 1),
        ("ra", 3), ("g", 1, 1, 0), ("bm", 2, 0), ("bm", 1, 0), ("ra", 2), ("g", 1, 2, 1), ("rb", 1, 1),
        ("g", 0, 3, 0), ("bm", 0, 1), ("g", 0, 1, 1), ("bm", 0, 0), ("f", 0, 1), ("rb", 2, 0), ("f", 1, 0),
        ("f", 1, 1), ("f", 0, 0), ("g", 1, 3, 0), ("rb", 1, 0), ("g", 1, 2, 0), ("g", 1, 3, 1), ("ra", 1),
        ("g", 0, 2, 1), ("eb",), ("g", 0, 3, 1), ("f", 2, 0), ("f", 2, 1), ("f", 3, 1), ("f", 3, 0), ("fb",), ("fa",),
    ),
    (
        ("own", 0), ("own", 1), ("g", 0, 0, 0), ("g", 0, 2, 0), ("bo", 0, 1), ("bo", 1, 1), ("bo", 2, 0),
        ("bo", 3, 1), ("bo", 2, 1), ("bo", 3, 0), ("g", 1, 1, 1), ("bo", 1, 0), ("g", 1, 2, 0), ("g", 1, 0, 0),
        ("g", 0, 3, 0), ("bo", 0, 0), ("bm", 3, 1), ("bm", 2, 1), ("g", 1, 0, 1), ("bm", 2, 0), ("rb", 2, 1),
        ("g", 0, 0, 1), ("bm", 0, 1), ("g", 1, 2, 1), ("g", 0, 1, 1), ("bm", 3, 0), ("g", 0, 3, 1), ("bm", 1, 1),
        ("bm", 0, 0), ("g", 1, 3, 0), ("rb", 3, 0), ("g", 0, 2, 1), ("rb", 3, 1), ("g", 1, 3, 1), ("ra", 3),
        ("bm", 1, 0), ("ra", 2), ("rb", 0, 1), ("f", 1, 1), ("f", 2, 1), ("rb", 0, 0), ("f", 3, 1), ("ra", 0),
        ("rb", 2, 0), ("f", 0, 0), ("f", 1, 0), ("eb",), ("f", 3, 0), ("f", 0, 1), ("f", 2, 0), ("fa",), ("fb",),
    ),
)
NN = (((1,), (0,)), ((), ()))
bf16 = jnp.bfloat16
f32 = jnp.float32


def dot(a, b, dims=NN):
    return lax.dot_general(a, b, dims, preferred_element_type=f32)


class Plan:
    def __init__(self, rows, sources):
        self.rows = rows
        self.sources = sources
        self.pair = 2 * sources
        self.panel_a = rows * 256 // 512
        self.sum_a = self.pair * 192 // 256


def fused_kernel(plan, counts_ref, cols_ref, dr_hbm, di_hbm, real_ref, imag_ref, fits_ref,
                 d, rows_out, rows_kept, rows_got, rows_all, own, panels, pt, sums_out, sums_got, sums, kept,
                 ya, line_a, line_b, yb, acc, total,
                 load_sem, rs_send, rs_recv, ra_send, ra_recv,
                 g_send, g_recv, xs_send, xs_recv, y_send, y_recv, la_send, la_recv, lb_send, lb_recv, yb_send, yb_recv):
    R, S, PAIR = plan.rows, plan.sources, plan.pair
    PA, SA = plan.panel_a, plan.sum_a
    me = lax.axis_index("row")
    core = lax.rem(me, 2)
    chip = me // 2
    y = lax.rem(chip, 2)
    z = chip // 2
    sibling = chip * 2 + (1 - core)

    def dev(k):
        return {"row": k * 2 + core}

    sib = {"row": sibling}

    def flip(k, m):
        kz, ky = k // 2, lax.rem(k, 2)
        mz, my = m // 2, lax.rem(m, 2)
        hz, lz = kz // 2, lax.rem(kz, 2)
        hm, lm = mz // 2, lax.rem(mz, 2)
        return (lax.rem(hz + hm, 2) * 2 + lax.rem(lz + lm, 2)) * 2 + lax.rem(ky + my, 2)

    def load(q, k):
        src = (dr_hbm, di_hbm)[q]
        return pltpu.make_async_copy(
            src.at[:, pl.ds(pl.multiple_of(k * 2 * R, 2 * R), 2 * R)], d.at[q, k], load_sem.at[q, k])

    @pl.loop(0, CHIPS)
    def _(i):
        k = flip(chip, CHIPS - 1 - i)
        load(0, k).start()
        load(1, k).start()

    def remote(src, dst, ssem, rsem, where):
        return pltpu.make_async_remote_copy(
            src_ref=src, dst_ref=dst, send_sem=ssem, recv_sem=rsem, device_id=where, device_id_type=MESH)

    barrier = pltpu.get_barrier_semaphore()
    pl.semaphore_signal(barrier, inc=1, device_id=sib, device_id_type=MESH)

    @pl.loop(1, CHIPS)
    def _(m):
        pl.semaphore_signal(barrier, inc=1, device_id=dev(flip(chip, m)), device_id_type=MESH)

    def chip_of(cols):
        return sum((cols >= t * 2 * R).astype(jnp.int32) for t in range(1, CHIPS))

    cols_row = cols_ref[...]
    cols_col = jnp.broadcast_to(cols_row.astype(f32), (S, S)).T.astype(jnp.int32)[:, :1]
    chip_row, chip_col = chip_of(cols_row), chip_of(cols_col)
    same = (jnp.broadcast_to(chip_row, (S, S)) == jnp.broadcast_to(chip_col, (S, S)))
    sub = lax.broadcasted_iota(jnp.int32, (S, S), 0)
    lane = lax.broadcasted_iota(jnp.int32, (S, S), 1)
    rank_row = jnp.sum(jnp.where(same & (sub < lane), 1.0, 0.0), axis=0, keepdims=True)
    rank_col = jnp.sum(jnp.where(same & (lane < sub), 1.0, 0.0), axis=1, keepdims=True)
    most = jnp.max(rank_row, axis=1, keepdims=True)
    fits_ref[0] = (most[0, 0] < SLOTS).astype(jnp.int32)
    slot_row = chip_row.astype(f32) * SLOTS + rank_row
    slot_col = chip_col.astype(f32) * SLOTS + rank_col
    k_iota = lax.broadcasted_iota(jnp.int32, (SLOTS, S), 0).astype(f32)
    mine = jnp.where(slot_row == k_iota + (chip * SLOTS).astype(f32), 1.0, 0.0).astype(bf16)
    at_row = me * R + lax.broadcasted_iota(jnp.int32, (S, R), 1)
    pick = dot(mine, jnp.where(cols_col == at_row, 1.0, 0.0).astype(bf16)).astype(bf16)
    spread = jnp.where(
        slot_col == lax.broadcasted_iota(jnp.int32, (S, CHIPS * SLOTS), 1).astype(f32), 1.0, 0.0).astype(bf16)

    half_other = pl.multiple_of((1 - core) * R, R)
    half_mine = pl.multiple_of(core * R, R)
    pl.semaphore_wait(barrier, CHIPS)

    def to_sibling_rows(k):
        return remote(rows_out.at[k], rows_got.at[k], rs_send.at[k], rs_recv.at[k], sib)

    parts = ((0, PA), (PA, R - PA))

    def to_owner_rows(k, part):
        off, size = parts[part]
        return remote(rows_kept.at[k, :, pl.ds(off, size)], rows_all.at[chip, :, pl.ds(off, size)],
                      ra_send.at[part, k], ra_recv.at[part, chip], dev(k))

    own[...] = jnp.zeros_like(own)
    total[...] = jnp.zeros_like(total)

    @pl.loop(0, CHIPS)
    def _(i):
        k = flip(chip, CHIPS - 1 - i)
        load(0, k).wait()
        load(1, k).wait()
        for q in range(2):
            rows_out[k, q * SLOTS:(q + 1) * SLOTS, :] = dot(pick, d[q, k, :, pl.ds(half_other, R)]).astype(bf16)
        to_sibling_rows(k).start()
        for q in range(2):
            rows_kept[k, q * SLOTS:(q + 1) * SLOTS, :] = dot(pick, d[q, k, :, pl.ds(half_mine, R)]).astype(bf16)

        @pl.when(i > 0)
        def _():
            last = flip(chip, CHIPS - i)
            to_sibling_rows(last).wait_recv()
            rows_kept[last] = rows_kept[last] + rows_got[last]
            to_owner_rows(last, 0).start()

    @pl.loop(0, CHIPS - 1)
    def _(i):
        to_owner_rows(flip(chip, CHIPS - 1 - i), 1).start()

    to_sibling_rows(chip).wait_recv()
    rows_all[chip] = rows_kept[chip] + rows_got[chip]

    @pl.loop(0, CHIPS)
    def _(k):
        at_col = k * 2 * R + lax.broadcasted_iota(jnp.int32, (2 * R, S), 0)
        take = jnp.where(cols_row == at_col, 1.0, 0.0).astype(bf16)
        own[0] += dot(d[0, k], take)
        own[1] += dot(d[1, k], take)

    w = jnp.zeros((1, S), f32)
    v = jnp.zeros((1, S), f32)
    for t in range(TILES):
        w = jnp.where(chip_row == t, counts_ref[chip, t].astype(f32), w)
        v = jnp.where(chip_row == t, counts_ref[t, chip].astype(f32), v)
    denom = jnp.maximum(w + v, 1.0)

    far = z // 2
    middle = z * (NZ - 1 - z) // 2
    at_end = middle == 0

    def line(u):
        return u + far * (NZ - 1 - 2 * u)

    def chip_at(u, s):
        return line(u) * 2 + (y if s == 0 else 1 - y)

    def turn(table, i):
        u, s = 0, 0
        for n in range(CHIPS):
            (ue, se), (um, sm) = table[0][n], table[1][n]
            here = (i == n).astype(jnp.int32)
            u += here * (ue + middle * (um - ue))
            s += here * (se + middle * (sm - se))
        return line(u) * 2 + y + s * (1 - 2 * y), s

    def table(kind):
        return tuple(tuple(t[1:] for t in row if t[0] == kind) for row in ORDER)

    across = {"row": (z * 2 + (1 - y)) * 2 + core}
    ROW_A, ROW_B = pl.ds(0, SA), pl.ds(SA, PAIR - SA)

    def scale(k):
        f = counts_ref[chip, k].astype(f32)
        b = counts_ref[k, chip].astype(f32)
        return jnp.full((1, 1), f, f32) / jnp.maximum(jnp.full((1, 1), f + b, f32), 1.0)

    def block_of(k, c, part):
        off, size = parts[part]
        return panels.at[k, pl.ds(pl.multiple_of(c * R + off, 16), size)]

    def garrived(k, c, part):
        remote(block_of(k, c, part), block_of(k, c, part), g_send.at[0, part, k], g_recv.at[part, k, c], sib).wait_recv()

    def y_copy(kz):
        return remote(sums.at[kz * 2 + (1 - y), ROW_A], ya.at[kz], y_send.at[kz], y_recv.at[kz], across)

    def sib_sum(k):
        return remote(sums_out.at[k], sums_got.at[k], xs_send.at[k], xs_recv.at[k], sib)

    def back(k, half):
        return scale(k) * (dot(pt[0], d[0, k, :, pl.ds(half, R)]) + dot(pt[1], d[1, k, :, pl.ds(half, R)]))

    class Tasks:
        def __init__(self, u):
            self.u = u
            self.sent = []
            self.ends = [w for w in (-1, 1) if 0 <= u + w]

        def toward(self, w):
            return {"row": chip_at(self.u + w, 0) * 2 + core}

        def came(self, w):
            return far if w > 0 else 1 - far

        def start(self, copy, *place):
            copy(*place).start()
            self.sent.append((copy, place))

        def panel_copy(self, u, s, part, way):
            k = chip_at(u, s)
            where = (sib, across, None)[min(3 - way, 2)] or self.toward(2 * way - 1)
            return remote(
                block_of(k, core, part), block_of(k, core, part), g_send.at[way, part, k], g_recv.at[part, k, core], where)

        def own(self, part):
            for w in self.ends:
                self.start(self.panel_copy, self.u, 0, part, (w + 1) // 2)
            self.start(self.panel_copy, self.u, 0, part, 2)
            self.start(self.panel_copy, self.u, 0, part, 3)

        def g(self, part, u, s):
            garrived(chip_at(u, s), core, part)
            ways = self.ends if u == self.u else [1 if u < self.u else -1]
            if part == 1 or s == 0:
                for w in ways:
                    if w in self.ends:
                        self.start(self.panel_copy, u, s, part, (w + 1) // 2)
            if part == 0 and s == 0:
                self.start(self.panel_copy, u, s, part, 2)
            self.start(self.panel_copy, u, s, part, 3)

        def a_copy(self, u, w):
            kz = line(u)
            return remote(sums.at[kz * 2 + y, ROW_A], line_a.at[self.came(w), kz], la_send.at[kz], la_recv.at[self.came(w), kz],
                          self.toward(w))

        def b_copy(self, u, s, w):
            k = chip_at(u, s)
            return remote(sums.at[k, ROW_B], line_b.at[self.came(w), k], lb_send.at[k], lb_recv.at[self.came(w), k],
                          self.toward(w))

        def with_a(self, value, kz, w):
            c = self.came(w)
            remote(line_a.at[c, kz], line_a.at[c, kz], la_send.at[kz], la_recv.at[c, kz], sib).wait_recv()
            return value + line_a[c, kz].astype(f32)

        def with_b(self, value, k, w):
            c = self.came(w)
            remote(line_b.at[c, k], line_b.at[c, k], lb_send.at[k], lb_recv.at[c, k], sib).wait_recv()
            return value + line_b[c, k].astype(f32)

        def ra(self, u):
            kz = line(u)
            w = 1 if u > self.u else -1
            y_copy(kz).wait_recv()
            value = kept[kz * 2 + y, :SA, :] + ya[kz].astype(f32)
            if -w in self.ends:
                value = self.with_a(value, kz, w)
            sums[kz * 2 + y, :SA, :] = value.astype(bf16)
            self.start(self.a_copy, u, w)

        def rb(self, u, s):
            k = chip_at(u, s)
            w = 1 if u > self.u else -1
            value = kept[k, SA:, :]
            if -w in self.ends:
                value = self.with_b(value, k, w)
            sums[k, SA:, :] = value.astype(bf16)
            self.start(self.b_copy, u, s, w)

        def ended_b(self, k):
            value = kept[k, SA:, :]
            for w in self.ends:
                value = self.with_b(value, k, -w)
            return value

        def yb_copy(self):
            return remote(sums.at[chip_at(self.u, 1), ROW_B], yb, yb_send.at[0], yb_recv.at[0], across)

        def eb(self):
            k = chip_at(self.u, 1)
            sums[k, SA:, :] = self.ended_b(k).astype(bf16)
            self.start(self.yb_copy)

        def fa(self):
            y_copy(z).wait_recv()
            value = kept[chip, :SA, :] + ya[z].astype(f32)
            for w in self.ends:
                value = self.with_a(value, z, -w)
            acc[:SA, :] = value

        def fb(self):
            value = self.ended_b(chip)
            self.yb_copy().wait_recv()
            acc[SA:, :] = value + yb[...].astype(f32)

    both = (Tasks(0), Tasks(1))

    def slots(kind):
        found = []
        for row in ORDER:
            ahead, lists = [], []
            for t in row:
                if t[0] in ("bo", "bm", "f"):
                    if t[0] == kind:
                        lists.append(ahead)
                    ahead = []
                elif t[0] != "own":
                    ahead.append(t)
            found.append(lists + [ahead])
        return found

    def run(lists, i):
        for u, row in enumerate(lists):
            for n in range(CHIPS):
                if row[n]:
                    @pl.when((i == n) & (at_end if u == 0 else middle == 1))
                    def _():
                        for t in row[n]:
                            getattr(both[u], t[0])(*t[1:])

    def run_all(lists):
        for u in range(2):
            @pl.when(at_end if u == 0 else middle == 1)
            def _():
                for t in lists[u]:
                    getattr(both[u], t[0])(*t[1:])

    for part, (off, size) in enumerate(parts):
        @pl.loop(1, CHIPS)
        def _(m):
            k = flip(chip, m)
            spot = rows_all.at[k, :, pl.ds(off, size)]
            remote(spot, spot, ra_send.at[part, k], ra_recv.at[part, k], dev(k)).wait_recv()

        for q in range(2):
            found = rows_all[:, q * SLOTS:(q + 1) * SLOTS, off:off + size].reshape(CHIPS * SLOTS, size)
            mirror = dot(spread, found).T
            block = (w * own[q, off:off + size] + v * mirror) / denom
            panels[chip, pl.ds(pl.multiple_of(half_mine + off, 128), size), q * S:(q + 1) * S] = block.astype(bf16)
            side = block.T.astype(bf16)
            pt[0, q * S:(q + 1) * S, off:off + size] = side
            pt[1, (1 - q) * S:(2 - q) * S, off:off + size] = side if q == 0 else -side
        run_all([[("own", part)], [("own", part)]])


    @pl.loop(0, CHIPS)
    def _(i):
        run(slots("bo"), i)
        k, _ = turn(table("bo"), i)
        sums_out[k] = back(k, half_other).astype(bf16)
        sib_sum(k).start()

    @pl.loop(0, CHIPS)
    def _(i):
        run(slots("bm"), i)
        k, other = turn(table("bm"), i)
        value = back(k, half_mine)
        sib_sum(k).wait_recv()
        value = value + sums_got[k].astype(f32)
        kept[k] = value

        @pl.when(other == 1)
        def _():
            sums[k, :SA, :] = value[:SA].astype(bf16)
            y_copy(k // 2).start()

    @pl.loop(0, CHIPS)
    def _(i):
        run(slots("f"), i)
        k, _ = turn(table("f"), i)
        for part in range(2):
            garrived(k, 1 - core, part)
        panel = panels[k]
        size = scale(k)
        for q in range(2):
            total[q] += size * dot(d[q, k], panel)

    run_all([row[CHIPS] for row in slots("f")])
    factor = -1.0 / math.sqrt(CHIPS * 2 * R)
    real_ref[...] = factor * (total[0, :, :S] - total[1, :, S:] + acc[:S, :].T)
    imag_ref[...] = factor * (total[0, :, S:] + total[1, :, :S] + acc[S:, :].T)

    @pl.loop(0, CHIPS)
    def _(k):
        to_sibling_rows(k).wait_send()
        sib_sum(k).wait_send()

    @pl.loop(1, CHIPS)
    def _(m):
        for part in range(2):
            to_owner_rows(flip(chip, m), part).wait_send()

    @pl.loop(0, NZ)
    def _(kz):
        y_copy(kz).wait_send()

    for u in range(2):
        @pl.when(at_end if u == 0 else middle == 1)
        def _():
            for copy, place in both[u].sent:
                copy(*place).wait_send()


def fused(data_real, data_imag, counts, source_cols):
    rows, width = data_real.shape
    S = source_cols.shape[0]
    plan = Plan(rows, S)
    pair, sa = plan.pair, plan.sum_a
    sb = pair - sa
    vmem = pl.BlockSpec(memory_space=pltpu.VMEM)
    smem = pl.BlockSpec(memory_space=pltpu.SMEM)
    hbm = pl.BlockSpec(memory_space=pl.ANY)
    dma = pltpu.SemaphoreType.DMA
    V = pltpu.VMEM

    def kernel(*refs):
        fused_kernel(plan, *refs)

    return pl.pallas_call(
        kernel,
        out_shape=(jax.ShapeDtypeStruct((rows, S), f32),) * 2 + (jax.ShapeDtypeStruct((1,), jnp.int32),),
        in_specs=[smem, vmem, hbm, hbm],
        out_specs=(vmem, vmem, smem),
        scratch_shapes=[
            V((2, CHIPS, rows, 2 * rows), bf16),
            V((CHIPS, 2 * SLOTS, rows), bf16), V((CHIPS, 2 * SLOTS, rows), bf16),
            V((CHIPS, 2 * SLOTS, rows), bf16), V((CHIPS, 2 * SLOTS, rows), bf16),
            V((2, rows, S), f32), V((CHIPS, 2 * rows, pair), bf16), V((2, pair, rows), bf16),
            V((CHIPS, pair, rows), bf16), V((CHIPS, pair, rows), bf16), V((CHIPS, pair, rows), bf16),
            V((CHIPS, pair, rows), f32),
            V((NZ, sa, rows), bf16), V((2, NZ, sa, rows), bf16), V((2, CHIPS, sb, rows), bf16), V((sb, rows), bf16),
            V((pair, rows), f32), V((2, rows, pair), f32),
            dma((2, CHIPS)), dma((CHIPS,)), dma((CHIPS,)), dma((2, CHIPS)), dma((2, CHIPS)),
            dma((4, 2, CHIPS)), dma((2, CHIPS, 2)), dma((CHIPS,)), dma((CHIPS,)), dma((NZ,)), dma((NZ,)),
            dma((NZ,)), dma((2, NZ)), dma((CHIPS,)), dma((2, CHIPS)), dma((1,)), dma((1,)),
        ],
        compiler_params=pltpu.CompilerParams(
            collective_id=0, has_side_effects=True, vmem_limit_bytes=56 << 20),
        cost_estimate=pl.CostEstimate(
            flops=8 * rows * width * pair, bytes_accessed=4 * rows * width, transcendentals=0),
    )(counts, source_cols.reshape(1, S), data_real, data_imag)


def gathered(x):
    return lax.all_gather(x, "row", axis=0, tiled=True)


def scattered(x):
    return lax.psum_scatter(x, "row", scatter_dimension=0, tiled=True)


def swapped(x):
    return lax.all_to_all(x, "row", 0, 0)


def gathered_by_swap(x):
    n = lax.axis_size("row")
    return swapped(jnp.broadcast_to(x[None], (n,) + x.shape)).reshape((-1,) + x.shape[1:])


def scattered_by_swap(x):
    n = lax.axis_size("row")
    return swapped(x.reshape((n, -1) + x.shape[1:])).astype(f32).sum(0)


def crowded(data_real, data_imag, counts, source_cols):
    return generic(data_real, data_imag, counts, source_cols, gathered_by_swap, scattered_by_swap)


def generic(data_real, data_imag, counts, source_cols, gathered=gathered, scattered=scattered):
    rows, width = data_real.shape
    sources = source_cols.shape[0]
    tile = width // TILES
    factor = -1.0 / math.sqrt(width)
    row0 = lax.axis_index("row") * rows
    table = counts.astype(jnp.float32)
    forward = lax.dynamic_index_in_dim(table, row0 // tile, 0, keepdims=False)
    backward = lax.dynamic_index_in_dim(table, row0 // tile, 1, keepdims=False)
    scale = jnp.repeat(forward / jnp.maximum(forward + backward, 1.0), tile)
    at_row = row0 + jnp.arange(rows, dtype=jnp.int32)
    pick_rows = (source_cols[:, None] == at_row[None, :]).astype(jnp.bfloat16)
    tn = (((0,), (1,)), ((), ()))
    picked = jnp.concatenate([dot(data_real, pick_rows, tn), dot(data_imag, pick_rows, tn)], axis=1)
    mirror = scattered(picked.astype(jnp.bfloat16))
    own = jnp.concatenate([jnp.take(data_real, source_cols, axis=1), jnp.take(data_imag, source_cols, axis=1)], axis=1)
    tiles = source_cols // tile
    w = jnp.tile(forward[tiles], 2)[None, :]
    v = jnp.tile(backward[tiles], 2)[None, :]
    panel = (w * own.astype(jnp.float32) + v * mirror.astype(jnp.float32)) / jnp.maximum(w + v, 1.0)
    panel = panel.astype(jnp.bfloat16)
    swap = lambda p: jnp.concatenate([-p[:, sources:], p[:, :sources]], axis=1)
    panels = gathered(panel)
    tt = (((0,), (0,)), ((), ()))
    back = scale[:, None] * (dot(data_real, panel, tt) + dot(data_imag, swap(panel), tt))
    back = scattered(back)
    steps = jnp.stack([
        s * (
            dot(data_real[:, t * tile : (t + 1) * tile], panels[t * tile : (t + 1) * tile])
            + dot(data_imag[:, t * tile : (t + 1) * tile], swap(panels[t * tile : (t + 1) * tile]))
        )
        for t, s in enumerate(scale[::tile])
    ])
    total = factor * (steps.sum(0) + back)
    return total[:, :sources], total[:, sources:]


def solution(mesh):
    n = mesh.shape["row"]

    def body(data_real, data_imag, counts, source_cols):
        rows = data_real.shape[0]
        if rows % 128 == 0 and n == 2 * CHIPS and data_real.shape[1] == n * rows and source_cols.shape[0] % 128 == 0:
            real, imag, fits = fused(data_real, data_imag, counts, source_cols)
            return lax.cond(
                fits[0] == 1, lambda *args: (real, imag), crowded, data_real, data_imag, counts, source_cols)
        return generic(data_real, data_imag, counts, source_cols)

    placed = (P(("freq", "row"), None), P(("freq", "row"), None), P(), P())
    return jax.shard_map(
        body,
        mesh=mesh,
        in_specs=placed,
        out_specs=(P(("freq", "row"), None), P(("freq", "row"), None)),
        check_vma=False,
    )
```

```python
import math

import jax
import jax.numpy as jnp
from jax import lax
from jax.experimental import pallas as pl
from jax.experimental.pallas import tpu as pltpu
from jax.experimental.layout import Layout, with_layout_constraint
from jax.sharding import PartitionSpec as P

TILES = 8
NZ = 4
CHIPS = 8
SLOTS = 32
MESH = pl.DeviceIdType.MESH
ORDER = (
    (
        ("own", 0), ("own", 1), ("bo", 3, 1), ("bo", 1, 1), ("bo", 2, 1), ("bo", 3, 0), ("g", 0, 1, 0), ("bo", 0, 0),
        ("bo", 0, 1), ("bo", 2, 0), ("bo", 1, 0), ("bm", 3, 1), ("g", 1, 0, 1), ("bm", 3, 0), ("bm", 2, 1),
        ("rb", 3, 1), ("rb", 2, 1), ("rb", 3, 0), ("bm", 1, 1), ("g", 0, 2, 0), ("g", 1, 1, 1), ("g", 0, 0, 1),
        ("ra", 3), ("g", 1, 1, 0), ("bm", 2, 0), ("bm", 1, 0), ("ra", 2), ("g", 1, 2, 1), ("rb", 1, 1),
        ("g", 0, 3, 0), ("bm", 0, 1), ("g", 0, 1, 1), ("bm", 0, 0), ("f", 0, 1), ("rb", 2, 0), ("f", 1, 0),
        ("f", 1, 1), ("f", 0, 0), ("g", 1, 3, 0), ("rb", 1, 0), ("g", 1, 2, 0), ("g", 1, 3, 1), ("ra", 1),
        ("g", 0, 2, 1), ("eb",), ("g", 0, 3, 1), ("f", 2, 0), ("f", 2, 1), ("f", 3, 1), ("f", 3, 0), ("fb",), ("fa",),
    ),
    (
        ("own", 0), ("own", 1), ("g", 0, 0, 0), ("g", 0, 2, 0), ("bo", 0, 1), ("bo", 1, 1), ("bo", 2, 0),
        ("bo", 3, 1), ("bo", 2, 1), ("bo", 3, 0), ("g", 1, 1, 1), ("bo", 1, 0), ("g", 1, 2, 0), ("g", 1, 0, 0),
        ("g", 0, 3, 0), ("bo", 0, 0), ("bm", 3, 1), ("bm", 2, 1), ("g", 1, 0, 1), ("bm", 2, 0), ("rb", 2, 1),
        ("g", 0, 0, 1), ("bm", 0, 1), ("g", 1, 2, 1), ("g", 0, 1, 1), ("bm", 3, 0), ("g", 0, 3, 1), ("bm", 1, 1),
        ("bm", 0, 0), ("g", 1, 3, 0), ("rb", 3, 0), ("g", 0, 2, 1), ("rb", 3, 1), ("g", 1, 3, 1), ("ra", 3),
        ("bm", 1, 0), ("ra", 2), ("rb", 0, 1), ("f", 1, 1), ("f", 2, 1), ("rb", 0, 0), ("f", 3, 1), ("ra", 0),
        ("rb", 2, 0), ("f", 0, 0), ("f", 1, 0), ("eb",), ("f", 3, 0), ("f", 0, 1), ("f", 2, 0), ("fa",), ("fb",),
    ),
)
NN = (((1,), (0,)), ((), ()))
bf16 = jnp.bfloat16
f32 = jnp.float32


def dot(a, b, dims=NN):
    return lax.dot_general(a, b, dims, preferred_element_type=f32)


class Plan:
    def __init__(self, rows, sources):
        self.rows = rows
        self.sources = sources
        self.pair = 2 * sources
        self.panel_a = rows * 256 // 512
        self.sum_a = self.pair * 192 // 256


def fused_kernel(plan, counts_ref, cols_ref, dr_hbm, di_hbm, out_ref, fits_ref,
                 d, rows_out, rows_kept, rows_got, rows_all, own, panels, pt, sums_out, sums_got, sums, kept,
                 ya, line_a, line_b, yb, acc, total,
                 load_sem, rs_send, rs_recv, ra_send, ra_recv,
                 g_send, g_recv, xs_send, xs_recv, y_send, y_recv, la_send, la_recv, lb_send, lb_recv, yb_send, yb_recv):
    R, S, PAIR = plan.rows, plan.sources, plan.pair
    PA, SA = plan.panel_a, plan.sum_a
    me = lax.axis_index("row")
    core = lax.rem(me, 2)
    chip = me // 2
    y = lax.rem(chip, 2)
    z = chip // 2
    sibling = chip * 2 + (1 - core)

    def dev(k):
        return {"row": k * 2 + core}

    sib = {"row": sibling}

    def flip(k, m):
        kz, ky = k // 2, lax.rem(k, 2)
        mz, my = m // 2, lax.rem(m, 2)
        hz, lz = kz // 2, lax.rem(kz, 2)
        hm, lm = mz // 2, lax.rem(mz, 2)
        return (lax.rem(hz + hm, 2) * 2 + lax.rem(lz + lm, 2)) * 2 + lax.rem(ky + my, 2)

    def load(q, k):
        src = (dr_hbm, di_hbm)[q]
        return pltpu.make_async_copy(
            src.at[:, pl.ds(pl.multiple_of(k * 2 * R, 2 * R), 2 * R)], d.at[q, k], load_sem.at[q, k])

    barrier = pltpu.get_barrier_semaphore()
    pl.semaphore_signal(barrier, inc=1, device_id=sib, device_id_type=MESH)

    @pl.loop(1, CHIPS)
    def _(m):
        pl.semaphore_signal(barrier, inc=1, device_id=dev(flip(chip, m)), device_id_type=MESH)

    @pl.loop(0, CHIPS)
    def _(i):
        k = flip(chip, CHIPS - 1 - i)
        load(0, k).start()
        load(1, k).start()

    def remote(src, dst, ssem, rsem, where):
        return pltpu.make_async_remote_copy(
            src_ref=src, dst_ref=dst, send_sem=ssem, recv_sem=rsem, device_id=where, device_id_type=MESH)

    def chip_of(cols):
        return sum((cols >= t * 2 * R).astype(jnp.int32) for t in range(1, CHIPS))

    cols_row = cols_ref[...]
    cols_col = jnp.broadcast_to(cols_row.astype(f32), (S, S)).T.astype(jnp.int32)[:, :1]
    chip_row, chip_col = chip_of(cols_row), chip_of(cols_col)
    same = (jnp.broadcast_to(chip_row, (S, S)) == jnp.broadcast_to(chip_col, (S, S)))
    sub = lax.broadcasted_iota(jnp.int32, (S, S), 0)
    lane = lax.broadcasted_iota(jnp.int32, (S, S), 1)
    rank_row = jnp.sum(jnp.where(same & (sub < lane), 1.0, 0.0), axis=0, keepdims=True)
    rank_col = jnp.sum(jnp.where(same & (lane < sub), 1.0, 0.0), axis=1, keepdims=True)
    most = jnp.max(rank_row, axis=1, keepdims=True)
    fits_ref[0] = (most[0, 0] < SLOTS).astype(jnp.int32)
    slot_row = chip_row.astype(f32) * SLOTS + rank_row
    slot_col = chip_col.astype(f32) * SLOTS + rank_col
    k_iota = lax.broadcasted_iota(jnp.int32, (SLOTS, S), 0).astype(f32)
    mine = jnp.where(slot_row == k_iota + (chip * SLOTS).astype(f32), 1.0, 0.0).astype(bf16)
    at_row = me * R + lax.broadcasted_iota(jnp.int32, (S, R), 1)
    pick = dot(mine, jnp.where(cols_col == at_row, 1.0, 0.0).astype(bf16)).astype(bf16)
    spread = jnp.where(
        slot_col == lax.broadcasted_iota(jnp.int32, (S, CHIPS * SLOTS), 1).astype(f32), 1.0, 0.0).astype(bf16)

    half_other = pl.multiple_of((1 - core) * R, R)
    half_mine = pl.multiple_of(core * R, R)
    pl.semaphore_wait(barrier, CHIPS)

    def to_sibling_rows(k):
        return remote(rows_out.at[k], rows_got.at[k], rs_send.at[k], rs_recv.at[k], sib)

    parts = ((0, PA), (PA, R - PA))

    def to_owner_rows(k, part):
        off, size = parts[part]
        return remote(rows_kept.at[k, :, pl.ds(off, size)], rows_all.at[chip, :, pl.ds(off, size)],
                      ra_send.at[part, k], ra_recv.at[part, chip], dev(k))

    own[...] = jnp.zeros_like(own)
    total[...] = jnp.zeros_like(total)

    @pl.loop(0, CHIPS)
    def _(i):
        k = flip(chip, CHIPS - 1 - i)
        load(0, k).wait()
        load(1, k).wait()
        for q in range(2):
            rows_out[k, q * SLOTS:(q + 1) * SLOTS, :] = dot(pick, d[q, k, :, pl.ds(half_other, R)]).astype(bf16)
        to_sibling_rows(k).start()
        for q in range(2):
            rows_kept[k, q * SLOTS:(q + 1) * SLOTS, :] = dot(pick, d[q, k, :, pl.ds(half_mine, R)]).astype(bf16)

        @pl.when(i > 0)
        def _():
            last = flip(chip, CHIPS - i)
            to_sibling_rows(last).wait_recv()
            rows_kept[last] = rows_kept[last] + rows_got[last]
            to_owner_rows(last, 0).start()

    @pl.loop(0, CHIPS - 1)
    def _(i):
        to_owner_rows(flip(chip, CHIPS - 1 - i), 1).start()

    to_sibling_rows(chip).wait_recv()
    rows_all[chip] = rows_kept[chip] + rows_got[chip]

    @pl.loop(0, CHIPS)
    def _(k):
        at_col = k * 2 * R + lax.broadcasted_iota(jnp.int32, (2 * R, S), 0)
        take = jnp.where(cols_row == at_col, 1.0, 0.0).astype(bf16)
        own[0] += dot(d[0, k], take)
        own[1] += dot(d[1, k], take)

    w = jnp.zeros((1, S), f32)
    v = jnp.zeros((1, S), f32)
    for t in range(TILES):
        w = jnp.where(chip_row == t, counts_ref[chip, t].astype(f32), w)
        v = jnp.where(chip_row == t, counts_ref[t, chip].astype(f32), v)
    denom = jnp.maximum(w + v, 1.0)

    far = z // 2
    middle = z * (NZ - 1 - z) // 2
    at_end = middle == 0

    def line(u):
        return u + far * (NZ - 1 - 2 * u)

    def chip_at(u, s):
        return line(u) * 2 + (y if s == 0 else 1 - y)

    def turn(table, i):
        u, s = 0, 0
        for n in range(CHIPS):
            (ue, se), (um, sm) = table[0][n], table[1][n]
            here = (i == n).astype(jnp.int32)
            u += here * (ue + middle * (um - ue))
            s += here * (se + middle * (sm - se))
        return line(u) * 2 + y + s * (1 - 2 * y), s

    def table(kind):
        return tuple(tuple(t[1:] for t in row if t[0] == kind) for row in ORDER)

    across = {"row": (z * 2 + (1 - y)) * 2 + core}
    ROW_A, ROW_B = pl.ds(0, SA), pl.ds(SA, PAIR - SA)

    def scale(k):
        f = counts_ref[chip, k].astype(f32)
        b = counts_ref[k, chip].astype(f32)
        return jnp.full((1, 1), f, f32) / jnp.maximum(jnp.full((1, 1), f + b, f32), 1.0)

    def block_of(k, c, part):
        off, size = parts[part]
        return panels.at[k, pl.ds(pl.multiple_of(c * R + off, 16), size)]

    def garrived(k, c, part):
        remote(block_of(k, c, part), block_of(k, c, part), g_send.at[0, part, k], g_recv.at[part, k, c], sib).wait_recv()

    def y_copy(kz):
        return remote(sums.at[kz * 2 + (1 - y), ROW_A], ya.at[kz], y_send.at[kz], y_recv.at[kz], across)

    def sib_sum(k):
        return remote(sums_out.at[k], sums_got.at[k], xs_send.at[k], xs_recv.at[k], sib)

    def back(k, half):
        return scale(k) * (dot(pt[0], d[0, k, :, pl.ds(half, R)]) + dot(pt[1], d[1, k, :, pl.ds(half, R)]))

    class Tasks:
        def __init__(self, u):
            self.u = u
            self.sent = []
            self.ends = [w for w in (-1, 1) if 0 <= u + w]

        def toward(self, w):
            return {"row": chip_at(self.u + w, 0) * 2 + core}

        def came(self, w):
            return far if w > 0 else 1 - far

        def start(self, copy, *place):
            copy(*place).start()
            self.sent.append((copy, place))

        def panel_copy(self, u, s, part, way):
            k = chip_at(u, s)
            where = (sib, across, None)[min(3 - way, 2)] or self.toward(2 * way - 1)
            return remote(
                block_of(k, core, part), block_of(k, core, part), g_send.at[way, part, k], g_recv.at[part, k, core], where)

        def own(self, part):
            for w in self.ends:
                self.start(self.panel_copy, self.u, 0, part, (w + 1) // 2)
            self.start(self.panel_copy, self.u, 0, part, 2)
            self.start(self.panel_copy, self.u, 0, part, 3)

        def g(self, part, u, s):
            garrived(chip_at(u, s), core, part)
            ways = self.ends if u == self.u else [1 if u < self.u else -1]
            if part == 1 or s == 0:
                for w in ways:
                    if w in self.ends:
                        self.start(self.panel_copy, u, s, part, (w + 1) // 2)
            if part == 0 and s == 0:
                self.start(self.panel_copy, u, s, part, 2)
            self.start(self.panel_copy, u, s, part, 3)

        def a_copy(self, u, w):
            kz = line(u)
            return remote(sums.at[kz * 2 + y, ROW_A], line_a.at[self.came(w), kz], la_send.at[kz], la_recv.at[self.came(w), kz],
                          self.toward(w))

        def b_copy(self, u, s, w):
            k = chip_at(u, s)
            return remote(sums.at[k, ROW_B], line_b.at[self.came(w), k], lb_send.at[k], lb_recv.at[self.came(w), k],
                          self.toward(w))

        def with_a(self, value, kz, w):
            c = self.came(w)
            remote(line_a.at[c, kz], line_a.at[c, kz], la_send.at[kz], la_recv.at[c, kz], sib).wait_recv()
            return value + line_a[c, kz].astype(f32)

        def with_b(self, value, k, w):
            c = self.came(w)
            remote(line_b.at[c, k], line_b.at[c, k], lb_send.at[k], lb_recv.at[c, k], sib).wait_recv()
            return value + line_b[c, k].astype(f32)

        def ra(self, u):
            kz = line(u)
            w = 1 if u > self.u else -1
            y_copy(kz).wait_recv()
            value = kept[kz * 2 + y, :SA, :] + ya[kz].astype(f32)
            if -w in self.ends:
                value = self.with_a(value, kz, w)
            sums[kz * 2 + y, :SA, :] = value.astype(bf16)
            self.start(self.a_copy, u, w)

        def rb(self, u, s):
            k = chip_at(u, s)
            w = 1 if u > self.u else -1
            value = kept[k, SA:, :]
            if -w in self.ends:
                value = self.with_b(value, k, w)
            sums[k, SA:, :] = value.astype(bf16)
            self.start(self.b_copy, u, s, w)

        def ended_b(self, k):
            value = kept[k, SA:, :]
            for w in self.ends:
                value = self.with_b(value, k, -w)
            return value

        def yb_copy(self):
            return remote(sums.at[chip_at(self.u, 1), ROW_B], yb, yb_send.at[0], yb_recv.at[0], across)

        def eb(self):
            k = chip_at(self.u, 1)
            sums[k, SA:, :] = self.ended_b(k).astype(bf16)
            self.start(self.yb_copy)

        def fa(self):
            y_copy(z).wait_recv()
            value = kept[chip, :SA, :] + ya[z].astype(f32)
            for w in self.ends:
                value = self.with_a(value, z, -w)
            acc[:SA, :] = value

        def fb(self):
            value = self.ended_b(chip)
            self.yb_copy().wait_recv()
            acc[SA:, :] = value + yb[...].astype(f32)

    both = (Tasks(0), Tasks(1))

    def slots(kind):
        found = []
        for row in ORDER:
            ahead, lists = [], []
            for t in row:
                if t[0] in ("bo", "bm", "f"):
                    if t[0] == kind:
                        lists.append(ahead)
                    ahead = []
                elif t[0] != "own":
                    ahead.append(t)
            found.append(lists + [ahead])
        return found

    def run(lists, i):
        for u, row in enumerate(lists):
            for n in range(CHIPS):
                if row[n]:
                    @pl.when((i == n) & (at_end if u == 0 else middle == 1))
                    def _():
                        for t in row[n]:
                            getattr(both[u], t[0])(*t[1:])

    def run_all(lists):
        for u in range(2):
            @pl.when(at_end if u == 0 else middle == 1)
            def _():
                for t in lists[u]:
                    getattr(both[u], t[0])(*t[1:])

    for part, (off, size) in enumerate(parts):
        @pl.loop(1, CHIPS)
        def _(m):
            k = flip(chip, m)
            spot = rows_all.at[k, :, pl.ds(off, size)]
            remote(spot, spot, ra_send.at[part, k], ra_recv.at[part, k], dev(k)).wait_recv()

        for q in range(2):
            found = rows_all[:, q * SLOTS:(q + 1) * SLOTS, off:off + size].reshape(CHIPS * SLOTS, size)
            mirror = dot(spread, found).T
            block = (w * own[q, off:off + size] + v * mirror) / denom
            panels[chip, pl.ds(pl.multiple_of(half_mine + off, 128), size), q * S:(q + 1) * S] = block.astype(bf16)
            side = block.T.astype(bf16)
            pt[0, q * S:(q + 1) * S, off:off + size] = side
            pt[1, (1 - q) * S:(2 - q) * S, off:off + size] = side if q == 0 else -side
        run_all([[("own", part)], [("own", part)]])


    @pl.loop(0, CHIPS)
    def _(i):
        run(slots("bo"), i)
        k, _ = turn(table("bo"), i)
        sums_out[k] = back(k, half_other).astype(bf16)
        sib_sum(k).start()

    @pl.loop(0, CHIPS)
    def _(i):
        run(slots("bm"), i)
        k, other = turn(table("bm"), i)
        value = back(k, half_mine)
        sib_sum(k).wait_recv()
        value = value + sums_got[k].astype(f32)
        kept[k] = value

        @pl.when(other == 1)
        def _():
            sums[k, :SA, :] = value[:SA].astype(bf16)
            y_copy(k // 2).start()

    @pl.loop(0, CHIPS)
    def _(i):
        run(slots("f"), i)
        k, _ = turn(table("f"), i)
        for part in range(2):
            garrived(k, 1 - core, part)
        panel = panels[k]
        size = scale(k)
        for q in range(2):
            total[q] += size * dot(d[q, k], panel)

    run_all([row[CHIPS] for row in slots("f")])
    out_ref[:, :S] = total[0, :, :S] - total[1, :, S:] + acc[:S, :].T
    out_ref[:, S:] = total[0, :, S:] + total[1, :, :S] + acc[S:, :].T

    @pl.loop(0, CHIPS)
    def _(k):
        to_sibling_rows(k).wait_send()
        sib_sum(k).wait_send()

    @pl.loop(1, CHIPS)
    def _(m):
        for part in range(2):
            to_owner_rows(flip(chip, m), part).wait_send()

    @pl.loop(0, NZ)
    def _(kz):
        y_copy(kz).wait_send()

    for u in range(2):
        @pl.when(at_end if u == 0 else middle == 1)
        def _():
            for copy, place in both[u].sent:
                copy(*place).wait_send()


def fused(data_real, data_imag, counts, source_cols):
    rows, width = data_real.shape
    S = source_cols.shape[0]
    plan = Plan(rows, S)
    pair, sa = plan.pair, plan.sum_a
    sb = pair - sa
    vmem = pl.BlockSpec(memory_space=pltpu.VMEM)
    smem = pl.BlockSpec(memory_space=pltpu.SMEM)
    hbm = pl.BlockSpec(memory_space=pl.ANY)
    dma = pltpu.SemaphoreType.DMA
    V = pltpu.VMEM

    def kernel(*refs):
        fused_kernel(plan, *refs)

    return pl.pallas_call(
        kernel,
        out_shape=(jax.ShapeDtypeStruct((rows, pair), f32), jax.ShapeDtypeStruct((1,), jnp.int32)),
        in_specs=[smem, vmem, hbm, hbm],
        out_specs=(vmem, smem),
        scratch_shapes=[
            V((2, CHIPS, rows, 2 * rows), bf16),
            V((CHIPS, 2 * SLOTS, rows), bf16), V((CHIPS, 2 * SLOTS, rows), bf16),
            V((CHIPS, 2 * SLOTS, rows), bf16), V((CHIPS, 2 * SLOTS, rows), bf16),
            V((2, rows, S), f32), V((CHIPS, 2 * rows, pair), bf16), V((2, pair, rows), bf16),
            V((CHIPS, pair, rows), bf16), V((CHIPS, pair, rows), bf16), V((CHIPS, pair, rows), bf16),
            V((CHIPS, pair, rows), f32),
            V((NZ, sa, rows), bf16), V((2, NZ, sa, rows), bf16), V((2, CHIPS, sb, rows), bf16), V((sb, rows), bf16),
            V((pair, rows), f32), V((2, rows, pair), f32),
            dma((2, CHIPS)), dma((CHIPS,)), dma((CHIPS,)), dma((2, CHIPS)), dma((2, CHIPS)),
            dma((4, 2, CHIPS)), dma((2, CHIPS, 2)), dma((CHIPS,)), dma((CHIPS,)), dma((NZ,)), dma((NZ,)),
            dma((NZ,)), dma((2, NZ)), dma((CHIPS,)), dma((2, CHIPS)), dma((1,)), dma((1,)),
        ],
        compiler_params=pltpu.CompilerParams(
            collective_id=0, has_side_effects=True, vmem_limit_bytes=56 << 20),
        cost_estimate=pl.CostEstimate(
            flops=8 * rows * width * pair, bytes_accessed=4 * rows * width, transcendentals=0),
    )(counts, source_cols.reshape(1, S), data_real, data_imag)


def gathered(x):
    return lax.all_gather(x, "row", axis=0, tiled=True)


def scattered(x):
    return lax.psum_scatter(x, "row", scatter_dimension=0, tiled=True)


def swapped(x):
    return lax.all_to_all(x, "row", 0, 0)


def gathered_by_swap(x):
    n = lax.axis_size("row")
    return swapped(jnp.broadcast_to(x[None], (n,) + x.shape)).reshape((-1,) + x.shape[1:])


def scattered_by_swap(x):
    n = lax.axis_size("row")
    return swapped(x.reshape((n, -1) + x.shape[1:])).astype(f32).sum(0)


def crowded(data_real, data_imag, counts, source_cols):
    both = generic(data_real, data_imag, counts, source_cols, gathered_by_swap, scattered_by_swap)
    return with_layout_constraint(both, Layout(major_to_minor=(0, 1)))


def generic(data_real, data_imag, counts, source_cols, gathered=gathered, scattered=scattered):
    rows, width = data_real.shape
    sources = source_cols.shape[0]
    tile = width // TILES
    row0 = lax.axis_index("row") * rows
    table = counts.astype(jnp.float32)
    forward = lax.dynamic_index_in_dim(table, row0 // tile, 0, keepdims=False)
    backward = lax.dynamic_index_in_dim(table, row0 // tile, 1, keepdims=False)
    scale = jnp.repeat(forward / jnp.maximum(forward + backward, 1.0), tile)
    at_row = row0 + jnp.arange(rows, dtype=jnp.int32)
    pick_rows = (source_cols[:, None] == at_row[None, :]).astype(jnp.bfloat16)
    tn = (((0,), (1,)), ((), ()))
    picked = jnp.concatenate([dot(data_real, pick_rows, tn), dot(data_imag, pick_rows, tn)], axis=1)
    mirror = scattered(picked.astype(jnp.bfloat16))
    own = jnp.concatenate([jnp.take(data_real, source_cols, axis=1), jnp.take(data_imag, source_cols, axis=1)], axis=1)
    tiles = source_cols // tile
    w = jnp.tile(forward[tiles], 2)[None, :]
    v = jnp.tile(backward[tiles], 2)[None, :]
    panel = (w * own.astype(jnp.float32) + v * mirror.astype(jnp.float32)) / jnp.maximum(w + v, 1.0)
    panel = panel.astype(jnp.bfloat16)
    swap = lambda p: jnp.concatenate([-p[:, sources:], p[:, :sources]], axis=1)
    panels = gathered(panel)
    tt = (((0,), (0,)), ((), ()))
    back = scale[:, None] * (dot(data_real, panel, tt) + dot(data_imag, swap(panel), tt))
    back = scattered(back)
    steps = jnp.stack([
        s * (
            dot(data_real[:, t * tile : (t + 1) * tile], panels[t * tile : (t + 1) * tile])
            + dot(data_imag[:, t * tile : (t + 1) * tile], swap(panels[t * tile : (t + 1) * tile]))
        )
        for t, s in enumerate(scale[::tile])
    ])
    return steps.sum(0) + back


def finished(both, width):
    factor = -1.0 / math.sqrt(width)
    sources = both.shape[1] // 2
    return factor * both[:, :sources], factor * both[:, sources:]


def solution(mesh):
    n = mesh.shape["row"]

    def body(data_real, data_imag, counts, source_cols):
        rows = data_real.shape[0]
        if rows % 128 == 0 and n == 2 * CHIPS and data_real.shape[1] == n * rows and source_cols.shape[0] % 128 == 0:
            both, fits = fused(data_real, data_imag, counts, source_cols)
            both = lax.cond(fits[0] == 1, lambda *args: both, crowded, data_real, data_imag, counts, source_cols)
            return finished(with_layout_constraint(both, Layout(major_to_minor=(0, 1))), data_real.shape[1])
        return finished(generic(data_real, data_imag, counts, source_cols), data_real.shape[1])

    placed = (P(("freq", "row"), None), P(("freq", "row"), None), P(), P())
    return jax.shard_map(
        body,
        mesh=mesh,
        in_specs=placed,
        out_specs=(P(("freq", "row"), None), P(("freq", "row"), None)),
        check_vma=False,
    )
```

```python
import math

import jax
import jax.numpy as jnp
from jax import lax
from jax.experimental import pallas as pl
from jax.experimental.pallas import tpu as pltpu
from jax.experimental.layout import Layout, with_layout_constraint
from jax.sharding import PartitionSpec as P

TILES = 8
NZ = 4
CHIPS = 8
SLOTS = 32
MESH = pl.DeviceIdType.MESH
ORDER = (
    (
        ("own", 0), ("own", 1), ("bo", 3, 1), ("bo", 1, 1), ("bo", 2, 1), ("bo", 3, 0), ("g", 0, 1, 0), ("bo", 0, 0),
        ("bo", 0, 1), ("bo", 2, 0), ("bo", 1, 0), ("bm", 3, 1), ("g", 1, 0, 1), ("bm", 3, 0), ("bm", 2, 1),
        ("rb", 3, 1), ("rb", 2, 1), ("rb", 3, 0), ("bm", 1, 1), ("g", 0, 2, 0), ("g", 1, 1, 1), ("g", 0, 0, 1),
        ("ra", 3), ("g", 1, 1, 0), ("bm", 2, 0), ("bm", 1, 0), ("ra", 2), ("g", 1, 2, 1), ("rb", 1, 1),
        ("g", 0, 3, 0), ("bm", 0, 1), ("g", 0, 1, 1), ("bm", 0, 0), ("f", 0, 1), ("rb", 2, 0), ("f", 1, 0),
        ("f", 1, 1), ("f", 0, 0), ("g", 1, 3, 0), ("rb", 1, 0), ("g", 1, 2, 0), ("g", 1, 3, 1), ("ra", 1),
        ("g", 0, 2, 1), ("eb",), ("g", 0, 3, 1), ("f", 2, 0), ("f", 2, 1), ("f", 3, 1), ("f", 3, 0), ("fb",), ("fa",),
    ),
    (
        ("own", 0), ("own", 1), ("g", 0, 0, 0), ("g", 0, 2, 0), ("bo", 0, 1), ("bo", 1, 1), ("bo", 2, 0),
        ("bo", 3, 1), ("bo", 2, 1), ("bo", 3, 0), ("g", 1, 1, 1), ("bo", 1, 0), ("g", 1, 2, 0), ("g", 1, 0, 0),
        ("g", 0, 3, 0), ("bo", 0, 0), ("bm", 3, 1), ("bm", 2, 1), ("g", 1, 0, 1), ("bm", 2, 0), ("rb", 2, 1),
        ("g", 0, 0, 1), ("bm", 0, 1), ("g", 1, 2, 1), ("g", 0, 1, 1), ("bm", 3, 0), ("g", 0, 3, 1), ("bm", 1, 1),
        ("bm", 0, 0), ("g", 1, 3, 0), ("rb", 3, 0), ("g", 0, 2, 1), ("rb", 3, 1), ("g", 1, 3, 1), ("ra", 3),
        ("bm", 1, 0), ("ra", 2), ("rb", 0, 1), ("f", 1, 1), ("f", 2, 1), ("rb", 0, 0), ("f", 3, 1), ("ra", 0),
        ("rb", 2, 0), ("f", 0, 0), ("f", 1, 0), ("eb",), ("f", 3, 0), ("f", 0, 1), ("f", 2, 0), ("fa",), ("fb",),
    ),
)
NN = (((1,), (0,)), ((), ()))
bf16 = jnp.bfloat16
f32 = jnp.float32


def dot(a, b, dims=NN):
    return lax.dot_general(a, b, dims, preferred_element_type=f32)


class Plan:
    def __init__(self, rows, sources):
        self.rows = rows
        self.sources = sources
        self.pair = 2 * sources
        self.panel_a = rows * 256 // 512
        self.sum_a = self.pair * 192 // 256


def fused_kernel(plan, counts_ref, cols_ref, dr_hbm, di_hbm, out_ref, fits_ref,
                 d, rows_out, rows_kept, rows_got, rows_all, own, panels, pt, sums_out, sums_got, sums, kept,
                 ya, line_a, line_b, yb, acc, total,
                 load_sem, rs_send, rs_recv, ra_send, ra_recv,
                 g_send, g_recv, xs_send, xs_recv, y_send, y_recv, la_send, la_recv, lb_send, lb_recv, yb_send, yb_recv):
    R, S, PAIR = plan.rows, plan.sources, plan.pair
    PA, SA = plan.panel_a, plan.sum_a
    me = lax.axis_index("row")
    core = lax.rem(me, 2)
    chip = me // 2
    y = lax.rem(chip, 2)
    z = chip // 2
    sibling = chip * 2 + (1 - core)

    def dev(k):
        return {"row": k * 2 + core}

    sib = {"row": sibling}

    def flip(k, m):
        kz, ky = k // 2, lax.rem(k, 2)
        mz, my = m // 2, lax.rem(m, 2)
        hz, lz = kz // 2, lax.rem(kz, 2)
        hm, lm = mz // 2, lax.rem(mz, 2)
        return (lax.rem(hz + hm, 2) * 2 + lax.rem(lz + lm, 2)) * 2 + lax.rem(ky + my, 2)

    def load(q, k):
        src = (dr_hbm, di_hbm)[q]
        return pltpu.make_async_copy(
            src.at[:, pl.ds(pl.multiple_of(k * 2 * R, 2 * R), 2 * R)], d.at[q, k], load_sem.at[q, k])

    barrier = pltpu.get_barrier_semaphore()
    pl.semaphore_signal(barrier, inc=1, device_id=sib, device_id_type=MESH)

    @pl.loop(1, CHIPS)
    def _(m):
        pl.semaphore_signal(barrier, inc=1, device_id=dev(flip(chip, m)), device_id_type=MESH)

    @pl.loop(0, 3)
    def _(i):
        k = flip(chip, CHIPS - 1 - i)
        load(0, k).start()
        load(1, k).start()

    def remote(src, dst, ssem, rsem, where):
        return pltpu.make_async_remote_copy(
            src_ref=src, dst_ref=dst, send_sem=ssem, recv_sem=rsem, device_id=where, device_id_type=MESH)

    def chip_of(cols):
        return sum((cols >= t * 2 * R).astype(jnp.int32) for t in range(1, CHIPS))

    cols_row = cols_ref[...]
    cols_col = jnp.broadcast_to(cols_row.astype(f32), (S, S)).T.astype(jnp.int32)[:, :1]
    chip_row, chip_col = chip_of(cols_row), chip_of(cols_col)
    same = (jnp.broadcast_to(chip_row, (S, S)) == jnp.broadcast_to(chip_col, (S, S)))
    sub = lax.broadcasted_iota(jnp.int32, (S, S), 0)
    lane = lax.broadcasted_iota(jnp.int32, (S, S), 1)
    rank_row = jnp.sum(jnp.where(same & (sub < lane), 1.0, 0.0), axis=0, keepdims=True)
    rank_col = jnp.sum(jnp.where(same & (lane < sub), 1.0, 0.0), axis=1, keepdims=True)
    most = jnp.max(rank_row, axis=1, keepdims=True)
    fits_ref[0] = (most[0, 0] < SLOTS).astype(jnp.int32)
    slot_row = chip_row.astype(f32) * SLOTS + rank_row
    slot_col = chip_col.astype(f32) * SLOTS + rank_col
    k_iota = lax.broadcasted_iota(jnp.int32, (SLOTS, S), 0).astype(f32)
    mine = jnp.where(slot_row == k_iota + (chip * SLOTS).astype(f32), 1.0, 0.0).astype(bf16)
    at_row = me * R + lax.broadcasted_iota(jnp.int32, (S, R), 1)
    pick = dot(mine, jnp.where(cols_col == at_row, 1.0, 0.0).astype(bf16)).astype(bf16)
    spread = jnp.where(
        slot_col == lax.broadcasted_iota(jnp.int32, (S, CHIPS * SLOTS), 1).astype(f32), 1.0, 0.0).astype(bf16)

    half_other = pl.multiple_of((1 - core) * R, R)
    half_mine = pl.multiple_of(core * R, R)
    pl.semaphore_wait(barrier, CHIPS)

    def to_sibling_rows(k):
        return remote(rows_out.at[k], rows_got.at[k], rs_send.at[k], rs_recv.at[k], sib)

    parts = ((0, PA), (PA, R - PA))

    def to_owner_rows(k, part):
        off, size = parts[part]
        return remote(rows_kept.at[k, :, pl.ds(off, size)], rows_all.at[chip, :, pl.ds(off, size)],
                      ra_send.at[part, k], ra_recv.at[part, chip], dev(k))

    own[...] = jnp.zeros_like(own)
    total[...] = jnp.zeros_like(total)

    @pl.loop(0, CHIPS)
    def _(i):
        k = flip(chip, CHIPS - 1 - i)
        load(0, k).wait()
        load(1, k).wait()

        @pl.when(i + 3 < CHIPS)
        def _():
            after = flip(chip, CHIPS - 4 - i)
            load(0, after).start()
            load(1, after).start()

        for q in range(2):
            rows_out[k, q * SLOTS:(q + 1) * SLOTS, :] = dot(pick, d[q, k, :, pl.ds(half_other, R)]).astype(bf16)
        to_sibling_rows(k).start()
        for q in range(2):
            rows_kept[k, q * SLOTS:(q + 1) * SLOTS, :] = dot(pick, d[q, k, :, pl.ds(half_mine, R)]).astype(bf16)

        @pl.when(i > 0)
        def _():
            last = flip(chip, CHIPS - i)
            to_sibling_rows(last).wait_recv()
            rows_kept[last] = rows_kept[last] + rows_got[last]
            to_owner_rows(last, 0).start()

    @pl.loop(0, CHIPS - 1)
    def _(i):
        to_owner_rows(flip(chip, CHIPS - 1 - i), 1).start()

    to_sibling_rows(chip).wait_recv()
    rows_all[chip] = rows_kept[chip] + rows_got[chip]

    @pl.loop(0, CHIPS)
    def _(k):
        at_col = k * 2 * R + lax.broadcasted_iota(jnp.int32, (2 * R, S), 0)
        take = jnp.where(cols_row == at_col, 1.0, 0.0).astype(bf16)
        own[0] += dot(d[0, k], take)
        own[1] += dot(d[1, k], take)

    w = jnp.zeros((1, S), f32)
    v = jnp.zeros((1, S), f32)
    for t in range(TILES):
        w = jnp.where(chip_row == t, counts_ref[chip, t].astype(f32), w)
        v = jnp.where(chip_row == t, counts_ref[t, chip].astype(f32), v)
    denom = jnp.maximum(w + v, 1.0)

    far = z // 2
    middle = z * (NZ - 1 - z) // 2
    at_end = middle == 0

    def line(u):
        return u + far * (NZ - 1 - 2 * u)

    def chip_at(u, s):
        return line(u) * 2 + (y if s == 0 else 1 - y)

    def turn(table, i):
        u, s = 0, 0
        for n in range(CHIPS):
            (ue, se), (um, sm) = table[0][n], table[1][n]
            here = (i == n).astype(jnp.int32)
            u += here * (ue + middle * (um - ue))
            s += here * (se + middle * (sm - se))
        return line(u) * 2 + y + s * (1 - 2 * y), s

    def table(kind):
        return tuple(tuple(t[1:] for t in row if t[0] == kind) for row in ORDER)

    across = {"row": (z * 2 + (1 - y)) * 2 + core}
    ROW_A, ROW_B = pl.ds(0, SA), pl.ds(SA, PAIR - SA)

    def scale(k):
        f = counts_ref[chip, k].astype(f32)
        b = counts_ref[k, chip].astype(f32)
        return jnp.full((1, 1), f, f32) / jnp.maximum(jnp.full((1, 1), f + b, f32), 1.0)

    def block_of(k, c, part):
        off, size = parts[part]
        return panels.at[k, pl.ds(pl.multiple_of(c * R + off, 16), size)]

    def garrived(k, c, part):
        remote(block_of(k, c, part), block_of(k, c, part), g_send.at[0, part, k], g_recv.at[part, k, c], sib).wait_recv()

    def y_copy(kz):
        return remote(sums.at[kz * 2 + (1 - y), ROW_A], ya.at[kz], y_send.at[kz], y_recv.at[kz], across)

    def sib_sum(k):
        return remote(sums_out.at[k], sums_got.at[k], xs_send.at[k], xs_recv.at[k], sib)

    def back(k, half):
        return scale(k) * (dot(pt[0], d[0, k, :, pl.ds(half, R)]) + dot(pt[1], d[1, k, :, pl.ds(half, R)]))

    class Tasks:
        def __init__(self, u):
            self.u = u
            self.sent = []
            self.ends = [w for w in (-1, 1) if 0 <= u + w]

        def toward(self, w):
            return {"row": chip_at(self.u + w, 0) * 2 + core}

        def came(self, w):
            return far if w > 0 else 1 - far

        def start(self, copy, *place):
            copy(*place).start()
            self.sent.append((copy, place))

        def panel_copy(self, u, s, part, way):
            k = chip_at(u, s)
            where = (sib, across, None)[min(3 - way, 2)] or self.toward(2 * way - 1)
            return remote(
                block_of(k, core, part), block_of(k, core, part), g_send.at[way, part, k], g_recv.at[part, k, core], where)

        def own(self, part):
            for w in self.ends:
                self.start(self.panel_copy, self.u, 0, part, (w + 1) // 2)
            self.start(self.panel_copy, self.u, 0, part, 2)
            self.start(self.panel_copy, self.u, 0, part, 3)

        def g(self, part, u, s):
            garrived(chip_at(u, s), core, part)
            ways = self.ends if u == self.u else [1 if u < self.u else -1]
            if part == 1 or s == 0:
                for w in ways:
                    if w in self.ends:
                        self.start(self.panel_copy, u, s, part, (w + 1) // 2)
            if part == 0 and s == 0:
                self.start(self.panel_copy, u, s, part, 2)
            self.start(self.panel_copy, u, s, part, 3)

        def a_copy(self, u, w):
            kz = line(u)
            return remote(sums.at[kz * 2 + y, ROW_A], line_a.at[self.came(w), kz], la_send.at[kz], la_recv.at[self.came(w), kz],
                          self.toward(w))

        def b_copy(self, u, s, w):
            k = chip_at(u, s)
            return remote(sums.at[k, ROW_B], line_b.at[self.came(w), k], lb_send.at[k], lb_recv.at[self.came(w), k],
                          self.toward(w))

        def with_a(self, value, kz, w):
            c = self.came(w)
            remote(line_a.at[c, kz], line_a.at[c, kz], la_send.at[kz], la_recv.at[c, kz], sib).wait_recv()
            return value + line_a[c, kz].astype(f32)

        def with_b(self, value, k, w):
            c = self.came(w)
            remote(line_b.at[c, k], line_b.at[c, k], lb_send.at[k], lb_recv.at[c, k], sib).wait_recv()
            return value + line_b[c, k].astype(f32)

        def ra(self, u):
            kz = line(u)
            w = 1 if u > self.u else -1
            y_copy(kz).wait_recv()
            value = kept[kz * 2 + y, :SA, :] + ya[kz].astype(f32)
            if -w in self.ends:
                value = self.with_a(value, kz, w)
            sums[kz * 2 + y, :SA, :] = value.astype(bf16)
            self.start(self.a_copy, u, w)

        def rb(self, u, s):
            k = chip_at(u, s)
            w = 1 if u > self.u else -1
            value = kept[k, SA:, :]
            if -w in self.ends:
                value = self.with_b(value, k, w)
            sums[k, SA:, :] = value.astype(bf16)
            self.start(self.b_copy, u, s, w)

        def ended_b(self, k):
            value = kept[k, SA:, :]
            for w in self.ends:
                value = self.with_b(value, k, -w)
            return value

        def yb_copy(self):
            return remote(sums.at[chip_at(self.u, 1), ROW_B], yb, yb_send.at[0], yb_recv.at[0], across)

        def eb(self):
            k = chip_at(self.u, 1)
            sums[k, SA:, :] = self.ended_b(k).astype(bf16)
            self.start(self.yb_copy)

        def fa(self):
            y_copy(z).wait_recv()
            value = kept[chip, :SA, :] + ya[z].astype(f32)
            for w in self.ends:
                value = self.with_a(value, z, -w)
            acc[:SA, :] = value

        def fb(self):
            value = self.ended_b(chip)
            self.yb_copy().wait_recv()
            acc[SA:, :] = value + yb[...].astype(f32)

    both = (Tasks(0), Tasks(1))

    def slots(kind):
        found = []
        for row in ORDER:
            ahead, lists = [], []
            for t in row:
                if t[0] in ("bo", "bm", "f"):
                    if t[0] == kind:
                        lists.append(ahead)
                    ahead = []
                elif t[0] != "own":
                    ahead.append(t)
            found.append(lists + [ahead])
        return found

    def run(lists, i):
        for u, row in enumerate(lists):
            for n in range(CHIPS):
                if row[n]:
                    @pl.when((i == n) & (at_end if u == 0 else middle == 1))
                    def _():
                        for t in row[n]:
                            getattr(both[u], t[0])(*t[1:])

    def run_all(lists):
        for u in range(2):
            @pl.when(at_end if u == 0 else middle == 1)
            def _():
                for t in lists[u]:
                    getattr(both[u], t[0])(*t[1:])

    for part, (off, size) in enumerate(parts):
        @pl.loop(1, CHIPS)
        def _(m):
            k = flip(chip, m)
            spot = rows_all.at[k, :, pl.ds(off, size)]
            remote(spot, spot, ra_send.at[part, k], ra_recv.at[part, k], dev(k)).wait_recv()

        for q in range(2):
            found = rows_all[:, q * SLOTS:(q + 1) * SLOTS, off:off + size].reshape(CHIPS * SLOTS, size)
            mirror = dot(spread, found).T
            block = (w * own[q, off:off + size] + v * mirror) / denom
            panels[chip, pl.ds(pl.multiple_of(half_mine + off, 128), size), q * S:(q + 1) * S] = block.astype(bf16)
            side = block.T.astype(bf16)
            pt[0, q * S:(q + 1) * S, off:off + size] = side
            pt[1, (1 - q) * S:(2 - q) * S, off:off + size] = side if q == 0 else -side
        run_all([[("own", part)], [("own", part)]])


    @pl.loop(0, CHIPS)
    def _(i):
        run(slots("bo"), i)
        k, _ = turn(table("bo"), i)
        sums_out[k] = back(k, half_other).astype(bf16)
        sib_sum(k).start()

    @pl.loop(0, CHIPS)
    def _(i):
        run(slots("bm"), i)
        k, other = turn(table("bm"), i)
        value = back(k, half_mine)
        sib_sum(k).wait_recv()
        value = value + sums_got[k].astype(f32)
        kept[k] = value

        @pl.when(other == 1)
        def _():
            sums[k, :SA, :] = value[:SA].astype(bf16)
            y_copy(k // 2).start()

    @pl.loop(0, CHIPS)
    def _(k):
        to_sibling_rows(k).wait_send()
        sib_sum(k).wait_send()

    @pl.loop(1, CHIPS)
    def _(m):
        for part in range(2):
            to_owner_rows(flip(chip, m), part).wait_send()

    @pl.loop(0, CHIPS)
    def _(i):
        run(slots("f"), i)
        k, _ = turn(table("f"), i)
        for part in range(2):
            garrived(k, 1 - core, part)
        panel = panels[k]
        size = scale(k)
        for q in range(2):
            total[q] += size * dot(d[q, k], panel)

    run_all([row[CHIPS] for row in slots("f")])
    out_ref[:, :S] = total[0, :, :S] - total[1, :, S:] + acc[:S, :].T
    out_ref[:, S:] = total[0, :, S:] + total[1, :, :S] + acc[S:, :].T

    @pl.loop(0, NZ)
    def _(kz):
        y_copy(kz).wait_send()

    for u in range(2):
        @pl.when(at_end if u == 0 else middle == 1)
        def _():
            for copy, place in both[u].sent:
                copy(*place).wait_send()


def fused(data_real, data_imag, counts, source_cols):
    rows, width = data_real.shape
    S = source_cols.shape[0]
    plan = Plan(rows, S)
    pair, sa = plan.pair, plan.sum_a
    sb = pair - sa
    vmem = pl.BlockSpec(memory_space=pltpu.VMEM)
    smem = pl.BlockSpec(memory_space=pltpu.SMEM)
    hbm = pl.BlockSpec(memory_space=pl.ANY)
    dma = pltpu.SemaphoreType.DMA
    V = pltpu.VMEM

    def kernel(*refs):
        fused_kernel(plan, *refs)

    return pl.pallas_call(
        kernel,
        out_shape=(jax.ShapeDtypeStruct((rows, pair), f32), jax.ShapeDtypeStruct((1,), jnp.int32)),
        in_specs=[smem, vmem, hbm, hbm],
        out_specs=(vmem, smem),
        scratch_shapes=[
            V((2, CHIPS, rows, 2 * rows), bf16),
            V((CHIPS, 2 * SLOTS, rows), bf16), V((CHIPS, 2 * SLOTS, rows), bf16),
            V((CHIPS, 2 * SLOTS, rows), bf16), V((CHIPS, 2 * SLOTS, rows), bf16),
            V((2, rows, S), f32), V((CHIPS, 2 * rows, pair), bf16), V((2, pair, rows), bf16),
            V((CHIPS, pair, rows), bf16), V((CHIPS, pair, rows), bf16), V((CHIPS, pair, rows), bf16),
            V((CHIPS, pair, rows), f32),
            V((NZ, sa, rows), bf16), V((2, NZ, sa, rows), bf16), V((2, CHIPS, sb, rows), bf16), V((sb, rows), bf16),
            V((pair, rows), f32), V((2, rows, pair), f32),
            dma((2, CHIPS)), dma((CHIPS,)), dma((CHIPS,)), dma((2, CHIPS)), dma((2, CHIPS)),
            dma((4, 2, CHIPS)), dma((2, CHIPS, 2)), dma((CHIPS,)), dma((CHIPS,)), dma((NZ,)), dma((NZ,)),
            dma((NZ,)), dma((2, NZ)), dma((CHIPS,)), dma((2, CHIPS)), dma((1,)), dma((1,)),
        ],
        compiler_params=pltpu.CompilerParams(
            collective_id=0, has_side_effects=True, vmem_limit_bytes=56 << 20),
        cost_estimate=pl.CostEstimate(
            flops=8 * rows * width * pair, bytes_accessed=4 * rows * width, transcendentals=0),
    )(counts, source_cols.reshape(1, S), data_real, data_imag)


def gathered(x):
    return lax.all_gather(x, "row", axis=0, tiled=True)


def scattered(x):
    return lax.psum_scatter(x, "row", scatter_dimension=0, tiled=True)


def swapped(x):
    return lax.all_to_all(x, "row", 0, 0)


def gathered_by_swap(x):
    n = lax.axis_size("row")
    return swapped(jnp.broadcast_to(x[None], (n,) + x.shape)).reshape((-1,) + x.shape[1:])


def scattered_by_swap(x):
    n = lax.axis_size("row")
    return swapped(x.reshape((n, -1) + x.shape[1:])).astype(f32).sum(0)


def crowded(data_real, data_imag, counts, source_cols):
    both = generic(data_real, data_imag, counts, source_cols, gathered_by_swap, scattered_by_swap)
    return with_layout_constraint(both, Layout(major_to_minor=(0, 1)))


def generic(data_real, data_imag, counts, source_cols, gathered=gathered, scattered=scattered):
    rows, width = data_real.shape
    sources = source_cols.shape[0]
    tile = width // TILES
    row0 = lax.axis_index("row") * rows
    table = counts.astype(jnp.float32)
    forward = lax.dynamic_index_in_dim(table, row0 // tile, 0, keepdims=False)
    backward = lax.dynamic_index_in_dim(table, row0 // tile, 1, keepdims=False)
    scale = jnp.repeat(forward / jnp.maximum(forward + backward, 1.0), tile)
    at_row = row0 + jnp.arange(rows, dtype=jnp.int32)
    pick_rows = (source_cols[:, None] == at_row[None, :]).astype(jnp.bfloat16)
    tn = (((0,), (1,)), ((), ()))
    picked = jnp.concatenate([dot(data_real, pick_rows, tn), dot(data_imag, pick_rows, tn)], axis=1)
    mirror = scattered(picked.astype(jnp.bfloat16))
    own = jnp.concatenate([jnp.take(data_real, source_cols, axis=1), jnp.take(data_imag, source_cols, axis=1)], axis=1)
    tiles = source_cols // tile
    w = jnp.tile(forward[tiles], 2)[None, :]
    v = jnp.tile(backward[tiles], 2)[None, :]
    panel = (w * own.astype(jnp.float32) + v * mirror.astype(jnp.float32)) / jnp.maximum(w + v, 1.0)
    panel = panel.astype(jnp.bfloat16)
    swap = lambda p: jnp.concatenate([-p[:, sources:], p[:, :sources]], axis=1)
    panels = gathered(panel)
    tt = (((0,), (0,)), ((), ()))
    back = scale[:, None] * (dot(data_real, panel, tt) + dot(data_imag, swap(panel), tt))
    back = scattered(back)
    steps = jnp.stack([
        s * (
            dot(data_real[:, t * tile : (t + 1) * tile], panels[t * tile : (t + 1) * tile])
            + dot(data_imag[:, t * tile : (t + 1) * tile], swap(panels[t * tile : (t + 1) * tile]))
        )
        for t, s in enumerate(scale[::tile])
    ])
    return steps.sum(0) + back


def finished(both, width):
    factor = -1.0 / math.sqrt(width)
    sources = both.shape[1] // 2
    return factor * both[:, :sources], factor * both[:, sources:]


def solution(mesh):
    n = mesh.shape["row"]

    def body(data_real, data_imag, counts, source_cols):
        rows = data_real.shape[0]
        if rows % 128 == 0 and n == 2 * CHIPS and data_real.shape[1] == n * rows and source_cols.shape[0] % 128 == 0:
            both, fits = fused(data_real, data_imag, counts, source_cols)
            both = lax.cond(fits[0] == 1, lambda *args: both, crowded, data_real, data_imag, counts, source_cols)
            return finished(with_layout_constraint(both, Layout(major_to_minor=(0, 1))), data_real.shape[1])
        return finished(generic(data_real, data_imag, counts, source_cols), data_real.shape[1])

    placed = (P(("freq", "row"), None), P(("freq", "row"), None), P(), P())
    return jax.shard_map(
        body,
        mesh=mesh,
        in_specs=placed,
        out_specs=(P(("freq", "row"), None), P(("freq", "row"), None)),
        check_vma=False,
    )
```
